512 devices in a mesh: gx: 32 (over z, x_hi), gy: 4 (over y), gz: 4 (over x_lo, core).
Axes of the slice: x: 4 (x_hi: 2, x_lo: 2; x = x_hi * 2 + x_lo), y: 4, z: 16, core: 2. Of those that a mesh axis runs over, the one named last changes fastest.
Arguments:
- tangent: bfloat16 [32, 128, 32, 512], P(None, 'gx', 'gy', 'gz'), may hold values from -130 to 130
- slopes: bfloat16 [32, 128, 32, 512], P(None, 'gx', 'gy', 'gz'), may hold values from -0.099609375 to 1.09375
- first_kernel: bfloat16 [27, 32, 32], replicated, may hold values from -0.21875 to 0.21875
- second_kernel: bfloat16 [27, 32, 32], replicated, may hold values from -0.21875 to 0.21875
Outputs:
- next_vector: float32 [32, 128, 32, 512], P(None, 'gx', 'gy', 'gz')
- jvp_norm: float32 [1], replicated
The draws below stay inside these ranges and needn't reach their ends.
All inputs are finite; a program needn't handle non-finite values.
Results may differ from the reference program's by a relative error of at most 0.0038.
Values may be sent and summed in bfloat16 or wider, within the bound.
No kernel may reach another device: no remote copies, remote signals or barrier semaphores. Data moves between devices by JAX's collectives and lax.ppermute only.
A program may use at most 192 MiB of HBM per device.

```python
import math
import jax
import jax.numpy as jnp

CH = 32
TAPS = 27
NX = 128
NY = 32
NZ = 512


def draw_tangent(key, part):
    key_chan, key_base = jax.random.split(key, 2)
    shape = (CH, NX, NY, NZ)
    chan = jnp.exp(jax.random.uniform(key_chan, (CH, 1, 1, 1), jnp.float32) * math.log(10.0))
    depth = jnp.arange(NX, dtype=jnp.float32).reshape(1, NX, 1, 1) / max(NX - 1, 1)
    base = jnp.clip(jax.random.normal(key_base, shape, jnp.float32), -6.0, 6.0)
    ramp = jnp.exp(math.log(3.0) * depth)
    values = base * chan * ramp * 0.2
    return jnp.clip(values, -130.0, 130.0).astype(jnp.bfloat16)


def block_scale(key, extent, cuts, low, top_value):
    def one(position, shards_of):
        draws = jax.random.uniform(jax.random.fold_in(jax.random.fold_in(key, 6), position), (shards_of,), jnp.float32, low / len(cuts), top_value / len(cuts))
        return jnp.repeat(jnp.exp(draws), extent[position] // shards_of).reshape((-1,) + (1,) * (len(extent) - position - 1))

    gain = one(*cuts[0])
    for cut in cuts[1:]:
        gain = gain * one(*cut)
    return gain


def normal_values(own_key, dims, deviation, most, kind=jnp.bfloat16):
    return jnp.clip(deviation * jax.random.normal(own_key, dims, jnp.float32), -most, most).astype(kind)


def setup_inputs(seed: int = 0) -> dict:
    keys = jax.random.split(jax.random.key(seed), 5)
    return {
        "tangent": draw_tangent(jax.random.fold_in(keys[4], 71), 0),
        "slopes": jnp.clip(-0.099609375 + 1.1933594 * jax.random.uniform(keys[1], (CH, NX, NY, NZ), jnp.float32) ** block_scale(keys[1], (CH, NX, NY, NZ), ((1, 32), (2, 4), (3, 4)), -0.2, 0.2), -0.099609375, 1.09375).astype(jnp.bfloat16),
        "first_kernel": normal_values(keys[2], (TAPS, CH, CH), (TAPS * CH) ** -0.5, 0.21875),
        "second_kernel": normal_values(keys[3], (TAPS, CH, CH), (TAPS * CH) ** -0.5, 0.21875),
    }


def convolve(field, kernel, adjoint):
    size_x, size_y, size_z = (field.shape[1], field.shape[2], field.shape[3])
    padded = jnp.pad(field, ((0, 0), (1, 1), (1, 1), (1, 1)))
    total = jnp.zeros((kernel.shape[1], size_x * size_y * size_z), jnp.float32)
    for a in (-1, 0, 1):
        for b in (-1, 0, 1):
            for c in (-1, 0, 1):
                tap = 9 * (a + 1) + 3 * (b + 1) + (c + 1)
                if adjoint:
                    sa, sb, sc = (1 - a, 1 - b, 1 - c)
                    matrix = kernel[tap].T
                else:
                    sa, sb, sc = (1 + a, 1 + b, 1 + c)
                    matrix = kernel[tap]
                piece = padded[:, sa:sa + size_x, sb:sb + size_y, sc:sc + size_z]
                total = total + jnp.dot(matrix, piece.reshape(piece.shape[0], -1), preferred_element_type=jnp.float32)
    return total.reshape(kernel.shape[1], size_x, size_y, size_z)

def reference(tangent, slopes, first_kernel, second_kernel):
    inner = convolve(tangent, first_kernel, False)
    hidden = (slopes.astype(jnp.float32) * inner).astype(jnp.bfloat16)
    image = convolve(hidden, second_kernel, False)
    image_low = image.astype(jnp.bfloat16)
    jvp_norm = jnp.sqrt(jnp.sum(image * image) + 1e-06)
    back = convolve(image_low, second_kernel, True)
    pulled = (slopes.astype(jnp.float32) * back).astype(jnp.bfloat16)
    next_vector = convolve(pulled, first_kernel, True) / jvp_norm
    return (next_vector, jvp_norm.reshape(1))
```

```python
import jax
import jax.numpy as jnp
from jax import lax
from jax.experimental import pallas as pl
from jax.experimental.pallas import tpu as pltpu
from jax.sharding import PartitionSpec as P

ALL = ("gx", "gy", "gz")
CH = 32
LANES = 128


def shift_pair(up, down, axis):
    ends = lax.axis_size(axis) - 1
    from_prev = lax.ppermute(up, axis, [(i, i + 1) for i in range(ends)])
    from_next = lax.ppermute(down, axis, [(i + 1, i) for i in range(ends)])
    return from_prev, from_next


def pack_kernel(f_ref, left_ref, right_ref):
    lane = lax.broadcasted_iota(jnp.int32, (CH, LANES), 1)

    def group(g, carry):
        left = jnp.zeros((CH, LANES), jnp.float32)
        right = jnp.zeros((CH, LANES), jnp.float32)
        for k in range(32):
            tile = f_ref[2 * g + k // 16, k % 16].astype(jnp.float32)
            rolled = pltpu.roll(tile, (4 * k + 4) % LANES, 1)
            right = jnp.where(lane // 4 == k, rolled, right)
            left = jnp.where(lane // 4 == (k + 1) % 32, rolled, left)
        left_ref[g] = left.astype(jnp.bfloat16)
        right_ref[g] = right.astype(jnp.bfloat16)
        return carry

    lax.fori_loop(0, left_ref.shape[0], group, 0)


def pack_edges(f):
    groups = f.shape[0] // 2
    out = jax.ShapeDtypeStruct((groups, CH, LANES), jnp.bfloat16)
    return pl.pallas_call(
        pack_kernel,
        out_shape=(out, out),
        compiler_params=pltpu.CompilerParams(vmem_limit_bytes=40 << 20),
        name="pack_edges",
    )(f)


def main_kernel(place, f_ref, rl_ref, rr_ref, w_ref, out_ref, sum_ref, h_ref, hid, img, pul):
    lane = lax.broadcasted_iota(jnp.int32, (CH, LANES), 1)

    def unpack(g, carry):
        rl = rl_ref[g].astype(jnp.float32)
        rr = rr_ref[g].astype(jnp.float32)
        low = (lane & 7) < 4
        even = jnp.where(low, rl, rr)
        odd = jnp.where(low, rr, rl)
        for k in range(32):
            tile = pltpu.roll(odd if k % 2 else even, (LANES - 4 * k - 4) % LANES, 1)
            h_ref[2 * g + k // 16, k % 16] = tile.astype(jnp.bfloat16)
        return carry

    lax.fori_loop(0, rl_ref.shape[0], unpack, 0)

    wide_lane = lax.broadcasted_iota(jnp.int32, (2 * CH, LANES), 1)

    def t_layer(t):
        return t + 2 + 4 * lax.shift_right_logical(t, 2)

    def s_layer(s):
        return s + 4 * lax.shift_right_logical(s + 2, 2)

    def field_rows(t, r):
        i = t_layer(t)
        a = f_ref[i, pl.ds(r, 4)].reshape(4 * CH, LANES)
        b = h_ref[i, pl.ds(r, 4)].reshape(4 * CH, LANES)
        return jnp.concatenate([a, b], axis=1)

    def scratch_rows(ref):
        def get(t, r):
            return ref[t, pl.ds(r, 4)].reshape(4 * CH, 2 * LANES)

        return get

    def conv_pair(which, get, m, r):
        rhs = jnp.concatenate([get(m + a, r) for a in range(3)], axis=0)
        g = jnp.dot(w_ref[which], rhs, preferred_element_type=jnp.float32)
        n = 2 * CH
        before = (g[:n, :LANES], g[:n, LANES:])
        mid = (g[n : 2 * n, :LANES], g[n : 2 * n, LANES:])
        after = (g[2 * n :, :LANES], g[2 * n :, LANES:])
        b0, b1 = (pltpu.roll(v, 1, 1) for v in before)
        a0, a1 = (pltpu.roll(v, LANES - 1, 1) for v in after)
        first = wide_lane == 0
        last = wide_lane == LANES - 1
        own = mid[0] + jnp.where(first, b1, b0) + jnp.where(last, a1, a0)
        halo = mid[1] + jnp.where(first, b0, b1) + jnp.where(last, a0, a1)
        return own, halo

    def slopes_at(m, r):
        i = s_layer(m)
        a = f_ref[i, pl.ds(r, 2)].reshape(2 * CH, LANES).astype(jnp.float32)
        b = h_ref[i, pl.ds(r, 2)].reshape(2 * CH, LANES).astype(jnp.float32)
        return a, b

    def store(ref, m, r, own, halo):
        ref[m, pl.ds(r, 2), :, :LANES] = own.astype(jnp.bfloat16).reshape(2, CH, LANES)
        ref[m, pl.ds(r, 2), :, LANES:] = halo.astype(jnp.bfloat16).reshape(2, CH, LANES)

    def stage_hidden(m, carry):
        for j in range(7):
            own, halo = conv_pair(0, field_rows, m, 2 * j)
            a, b = slopes_at(m, 2 * j + 1)
            store(hid, m, 2 * j, a * own, b * halo)
        return carry

    lax.fori_loop(0, 10, stage_hidden, 0)

    gx, gy, gz = place[0], place[1], place[2]
    nx, ny, nz = place[3], place[4], place[5]
    halo_lane = jnp.where(
        wide_lane < LANES // 2,
        jnp.where(gz < nz, 1.0, 0.0),
        jnp.where(gz > 0, 1.0, 0.0),
    )
    sum_ref[...] = jnp.zeros_like(sum_ref)

    def stage_image(m, carry):
        x_in = ((m >= 2) | (gx > 0)) & ((m < 6) | (gx < nx))
        x_own = (m >= 2) & (m < 6)
        for j in range(6):
            own, halo = conv_pair(1, scratch_rows(hid), m, 2 * j)
            keep = x_in
            if j < 1:
                keep = keep & (gy > 0)
            if j > 4:
                keep = keep & (gy < ny)
            scale = jnp.where(keep, 1.0, 0.0)
            store(img, m, 2 * j, own * scale, halo * (halo_lane * scale))
            if 1 <= j <= 4:
                square = own * own * jnp.where(x_own, 1.0, 0.0)
                part = square[0:8]
                for q in range(1, 8):
                    part = part + square[8 * q : 8 * q + 8]
                sum_ref[...] += part
        return carry

    lax.fori_loop(0, 8, stage_image, 0)

    def stage_pulled(m, carry):
        for j in range(5):
            own, halo = conv_pair(2, scratch_rows(img), m, 2 * j)
            a, b = slopes_at(m + 2, 2 * j + 3)
            store(pul, m, 2 * j, a * own, b * halo)
        return carry

    lax.fori_loop(0, 6, stage_pulled, 0)

    def stage_out(m, carry):
        for j in range(4):
            own, halo = conv_pair(3, scratch_rows(pul), m, 2 * j)
            out_ref[m, pl.ds(2 * j, 2)] = own.reshape(2, CH, LANES)
        return carry

    lax.fori_loop(0, 4, stage_out, 0)


def all_convs(place, f, rl, rr, weights):
    layers, rows = f.shape[0], f.shape[1]
    return pl.pallas_call(
        main_kernel,
        out_shape=(
            jax.ShapeDtypeStruct((4, 8, CH, LANES), jnp.float32),
            jax.ShapeDtypeStruct((8, LANES), jnp.float32),
        ),
        in_specs=[pl.BlockSpec(memory_space=pltpu.SMEM)]
        + [pl.BlockSpec(memory_space=pltpu.VMEM)] * 4,
        scratch_shapes=[
            pltpu.VMEM((layers, rows, CH, LANES), jnp.bfloat16),
            pltpu.VMEM((10, 14, CH, 2 * LANES), jnp.bfloat16),
            pltpu.VMEM((8, 12, CH, 2 * LANES), jnp.bfloat16),
            pltpu.VMEM((6, 10, CH, 2 * LANES), jnp.bfloat16),
        ],
        compiler_params=pltpu.CompilerParams(vmem_limit_bytes=48 << 20),
        name="all_convs",
    )(place, f, rl, rr, weights)


def pair_matrix(kernel):
    taps = kernel.reshape(3, 3, 3, CH, CH)
    none = ((0, 0), (0, 0), (0, 0), (0, 0))
    top = jnp.pad(taps, (none[0], (0, 1)) + none[:3])
    low = jnp.pad(taps, (none[0], (1, 0)) + none[:3])
    both = jnp.stack([top, low])
    return both.transpose(3, 0, 4, 1, 2, 5).reshape(6 * CH, 12 * CH)


def on_device(tangent, slopes, first_kernel, second_kernel):
    t = tangent.transpose(1, 2, 0, 3)
    s = slopes.transpose(1, 2, 0, 3)
    mine = jnp.concatenate([s[0:3], t, s[3:4]], axis=0)
    from_prev, from_next = shift_pair(mine[1:8], mine[0:7], "gx")
    deep = jnp.concatenate([from_prev, mine, from_next], axis=0)
    above, below = shift_pair(deep[:, 4:8], deep[:, 0:4], "gy")
    f = jnp.concatenate([above, deep, below], axis=1)
    left_edge, right_edge = pack_edges(f)
    rl, rr = shift_pair(right_edge, left_edge, "gz")

    adjoint = lambda k: k[::-1].transpose(0, 2, 1)
    weights = jnp.stack(
        [
            pair_matrix(first_kernel),
            pair_matrix(second_kernel),
            pair_matrix(adjoint(second_kernel)),
            pair_matrix(adjoint(first_kernel)),
        ]
    )
    place = jnp.stack(
        [lax.axis_index(a) for a in ALL] + [jnp.int32(lax.axis_size(a) - 1) for a in ALL]
    ).astype(jnp.int32)
    result, squares = all_convs(place, f, rl, rr, weights)

    part = jnp.sum(squares, axis=0, keepdims=True)
    for axes in (("gy", "gz"), "gx"):
        count = lax.axis_size(axes)
        spread = jnp.broadcast_to(part, (count, LANES))
        part = jnp.sum(lax.all_to_all(spread, axes, 0, 0, tiled=True), axis=0, keepdims=True)
    jvp_norm = jnp.sqrt(jnp.sum(part) + 1e-06)
    next_vector = result.transpose(2, 0, 1, 3) / jvp_norm
    return (next_vector, jvp_norm.reshape(1))


def solution(mesh):
    return jax.shard_map(
        on_device,
        mesh=mesh,
        in_specs=(P(None, "gx", "gy", "gz"), P(None, "gx", "gy", "gz"), P(), P()),
        out_specs=(P(None, "gx", "gy", "gz"), P()),
        check_vma=False,
    )
```

```python
import jax
import jax.numpy as jnp
from jax import lax
from jax.experimental import pallas as pl
from jax.experimental.pallas import tpu as pltpu
from jax.sharding import PartitionSpec as P

ALL = ("gx", "gy", "gz")
CH = 32
LANES = 128


def shift_pair(up, down, axis):
    ends = lax.axis_size(axis) - 1
    from_prev = lax.ppermute(up, axis, [(i, i + 1) for i in range(ends)])
    from_next = lax.ppermute(down, axis, [(i + 1, i) for i in range(ends)])
    return from_prev, from_next


def pack_kernel(f_ref, left_ref, right_ref):
    lane = lax.broadcasted_iota(jnp.int32, (CH, LANES), 1)
    low = (lane & 7) < 4

    def edges(layer):
        tile = jnp.zeros((CH, LANES), jnp.float32)
        for row in range(16):
            slot = 8 * (row % 2) + row // 2
            rolled = pltpu.roll(f_ref[layer, row].astype(jnp.float32), (8 * slot + 4) % LANES, 1)
            tile = jnp.where(lane // 8 == slot, rolled, tile)
        return tile

    def group(g, carry):
        one, two = edges(2 * g), edges(2 * g + 1)
        right_ref[g] = jnp.where(low, one, pltpu.roll(two, 4, 1)).astype(jnp.bfloat16)
        left_ref[g] = jnp.where(low, pltpu.roll(two, LANES - 4, 1), one).astype(jnp.bfloat16)
        return carry

    lax.fori_loop(0, left_ref.shape[0], group, 0)


def pack_edges(f):
    groups = f.shape[0] // 2
    out = jax.ShapeDtypeStruct((groups, CH, LANES), jnp.bfloat16)
    return pl.pallas_call(
        pack_kernel,
        out_shape=(out, out),
        compiler_params=pltpu.CompilerParams(vmem_limit_bytes=40 << 20),
        name="pack_edges",
    )(f)


def roll(v, shift):
    return pltpu.roll(v, shift % LANES, 1)


def main_kernel(
    place, f_ref, rl_ref, rr_ref, w_ref, out_ref, sum_ref, edge, t_h, hid, hid_h, img, img_h, pul, pul_h
):
    lane = lax.broadcasted_iota(jnp.int32, (CH, LANES), 1)
    low = (lane & 7) < 4

    def unpack(g, carry):
        rl = rl_ref[g].astype(jnp.float32)
        rr = rr_ref[g].astype(jnp.float32)
        edge[2 * g] = jnp.where(low, rl, rr)
        edge[2 * g + 1] = jnp.where(low, roll(rl, -4), roll(rr, 4))
        return carry

    lax.fori_loop(0, rl_ref.shape[0], unpack, 0)

    def t_layer(t):
        return t + 2 + 4 * lax.shift_right_logical(t, 2)

    def s_layer(s):
        return s + 4 * lax.shift_right_logical(s + 2, 2)

    def t_halo(t, carry):
        tile = edge[t_layer(t)]
        for q, shift in enumerate((0, 64, -8, 56)):
            t_h[t, q * CH : (q + 1) * CH] = roll(tile, shift).astype(jnp.bfloat16)
        return carry

    lax.fori_loop(0, 12, t_halo, 0)

    wide = lax.broadcasted_iota(jnp.int32, (2 * CH, LANES), 1)
    wide8 = wide & 7
    first = wide == 0
    n = 2 * CH

    def convolve_layer(which, get, get_halo, m, pairs, put, put_halo):
        def columns(p):
            if p < 0:
                return jnp.concatenate([get_halo(m + a) for a in range(3)], axis=0)
            return jnp.concatenate([get(m + a, 2 * p) for a in range(3)], axis=0)

        cross = None
        halo = None
        tiles = list(range(-1, pairs))
        for start in range(0, len(tiles), 2):
            here = tiles[start : start + 2]
            rhs = jnp.concatenate([columns(p) for p in here], axis=1)
            g = jnp.dot(w_ref[which], rhs, preferred_element_type=jnp.float32)
            for k, p in enumerate(here):
                part = g[:, k * LANES : (k + 1) * LANES]
                before = roll(part[:n], 1)
                after = roll(part[2 * n :], -1)
                if p < 0:
                    cross = jnp.where(wide8 == 4, before, after)
                    halo = (
                        part[n : 2 * n]
                        + jnp.where(wide8 == 4, 0.0, before)
                        + jnp.where(wide8 == 3, 0.0, after)
                    )
                    continue
                mine = roll(cross, -(8 * p + 4))
                own = (
                    part[n : 2 * n]
                    + jnp.where(first, mine, before)
                    + jnp.where(wide == LANES - 1, mine, after)
                )
                put(p, own)
                if put_halo is not None:
                    give = roll(jnp.where(first, before, after), 8 * p + 4)
                    halo = halo + jnp.where((wide == 8 * p + 3) | (wide == 8 * p + 4), give, 0.0)
        if put_halo is not None:
            put_halo(halo)

    def store_halo(ref, m, v):
        for q, piece in enumerate((v[:CH], v[CH:], roll(v[:CH], -8), roll(v[CH:], -8))):
            ref[m, q * CH : (q + 1) * CH] = piece.astype(jnp.bfloat16)

    def store(ref, m, p, v):
        ref[m, pl.ds(2 * p, 2)] = v.astype(jnp.bfloat16).reshape(2, CH, LANES)

    def scaled(ref, ref_h, s, row):
        i = s_layer(s)

        def put(m):
            def own(p, v):
                slope = f_ref[i, pl.ds(2 * p + row, 2)].reshape(2 * CH, LANES)
                store(ref, m, p, slope.astype(jnp.float32) * v)

            return own

        def put_halo(m):
            def halo(v):
                tile = edge[i]
                q = row // 2
                slope = jnp.concatenate([roll(tile, 64 - 8 * q), roll(tile, -8 * (q + 1))], axis=0)
                store_halo(ref_h, m, slope * v)

            return halo

        return put, put_halo

    def rows_of(ref):
        return lambda t, r: ref[t, pl.ds(r, 4)].reshape(4 * CH, LANES)

    def field_rows(t, r):
        return f_ref[t_layer(t), pl.ds(r, 4)].reshape(4 * CH, LANES)

    def stage_hidden(m, carry):
        put, put_halo = scaled(hid, hid_h, m, 1)
        convolve_layer(0, field_rows, lambda t: t_h[t], m, 7, put(m), put_halo(m))
        return carry

    lax.fori_loop(0, 10, stage_hidden, 0)

    gx, gy, gz = place[0], place[1], place[2]
    nx, ny, nz = place[3], place[4], place[5]
    top_in = jnp.where(gy > 0, 1.0, 0.0)
    low_in = jnp.where(gy < ny, 1.0, 0.0)
    halo_in = jnp.where(wide8 < 4, jnp.where(gz > 0, 1.0, 0.0), jnp.where(gz < nz, 1.0, 0.0))
    halo_in = jnp.where(wide < 8, halo_in * top_in, halo_in)
    halo_in = jnp.where(wide >= 40, halo_in * low_in, halo_in)
    sum_ref[...] = jnp.zeros_like(sum_ref)

    def stage_image(m, carry):
        x_in = jnp.where(((m >= 2) | (gx > 0)) & ((m < 6) | (gx < nx)), 1.0, 0.0)
        x_own = jnp.where((m >= 2) & (m < 6), 1.0, 0.0)

        def put(p, v):
            keep = x_in * (top_in if p == 0 else low_in if p == 5 else 1.0)
            store(img, m, p, v * keep)
            if 1 <= p <= 4:
                square = v * v * x_own
                part = square[0:8]
                for q in range(1, 8):
                    part = part + square[8 * q : 8 * q + 8]
                sum_ref[...] += part

        def put_halo(v):
            store_halo(img_h, m, v * (halo_in * x_in))

        convolve_layer(1, rows_of(hid), lambda t: hid_h[t], m, 6, put, put_halo)
        return carry

    lax.fori_loop(0, 8, stage_image, 0)

    def stage_pulled(m, carry):
        put, put_halo = scaled(pul, pul_h, m + 2, 3)
        convolve_layer(2, rows_of(img), lambda t: img_h[t], m, 5, put(m), put_halo(m))
        return carry

    lax.fori_loop(0, 6, stage_pulled, 0)

    def stage_out(m, carry):
        def put(p, v):
            out_ref[m, pl.ds(2 * p, 2)] = v.reshape(2, CH, LANES)

        convolve_layer(3, rows_of(pul), lambda t: pul_h[t], m, 4, put, None)
        return carry

    lax.fori_loop(0, 4, stage_out, 0)


def all_convs(place, f, rl, rr, weights):
    layers = f.shape[0]

    def field(deep, rows):
        return [
            pltpu.VMEM((deep, rows, CH, LANES), jnp.bfloat16),
            pltpu.VMEM((deep, 4 * CH, LANES), jnp.bfloat16),
        ]

    return pl.pallas_call(
        main_kernel,
        out_shape=(
            jax.ShapeDtypeStruct((4, 8, CH, LANES), jnp.float32),
            jax.ShapeDtypeStruct((8, LANES), jnp.float32),
        ),
        in_specs=[pl.BlockSpec(memory_space=pltpu.SMEM)]
        + [pl.BlockSpec(memory_space=pltpu.VMEM)] * 4,
        scratch_shapes=[
            pltpu.VMEM((layers, CH, LANES), jnp.float32),
            pltpu.VMEM((12, 4 * CH, LANES), jnp.bfloat16),
        ]
        + field(10, 14)
        + field(8, 12)
        + field(6, 10),
        compiler_params=pltpu.CompilerParams(vmem_limit_bytes=48 << 20),
        name="all_convs",
    )(place, f, rl, rr, weights)


def pair_matrix(kernel):
    taps = kernel.reshape(3, 3, 3, CH, CH)
    none = ((0, 0), (0, 0), (0, 0), (0, 0))
    top = jnp.pad(taps, (none[0], (0, 1)) + none[:3])
    low = jnp.pad(taps, (none[0], (1, 0)) + none[:3])
    both = jnp.stack([top, low])
    return both.transpose(3, 0, 4, 1, 2, 5).reshape(6 * CH, 12 * CH)


def on_device(tangent, slopes, first_kernel, second_kernel):
    t = tangent.transpose(1, 2, 0, 3)
    s = slopes.transpose(1, 2, 0, 3)
    mine = jnp.concatenate([s[0:3], t, s[3:4]], axis=0)
    from_prev, from_next = shift_pair(mine[1:8], mine[0:7], "gx")
    deep = jnp.concatenate([from_prev, mine, from_next], axis=0)
    above, below = shift_pair(deep[:, 4:8], deep[:, 0:4], "gy")
    f = jnp.concatenate([above, deep, below], axis=1)
    left_edge, right_edge = pack_edges(f)
    rl, rr = shift_pair(right_edge, left_edge, "gz")

    adjoint = lambda k: k[::-1].transpose(0, 2, 1)
    weights = jnp.stack(
        [
            pair_matrix(first_kernel),
            pair_matrix(second_kernel),
            pair_matrix(adjoint(second_kernel)),
            pair_matrix(adjoint(first_kernel)),
        ]
    )
    place = jnp.stack(
        [lax.axis_index(a) for a in ALL] + [jnp.int32(lax.axis_size(a) - 1) for a in ALL]
    ).astype(jnp.int32)
    result, squares = all_convs(place, f, rl, rr, weights)

    part = jnp.sum(squares, axis=0, keepdims=True)
    for axes in (("gy", "gz"), "gx"):
        count = lax.axis_size(axes)
        spread = jnp.broadcast_to(part, (count, LANES))
        part = jnp.sum(lax.all_to_all(spread, axes, 0, 0, tiled=True), axis=0, keepdims=True)
    jvp_norm = jnp.sqrt(jnp.sum(part) + 1e-06)
    next_vector = result.transpose(2, 0, 1, 3) / jvp_norm
    return (next_vector, jvp_norm.reshape(1))


def solution(mesh):
    return jax.shard_map(
        on_device,
        mesh=mesh,
        in_specs=(P(None, "gx", "gy", "gz"), P(None, "gx", "gy", "gz"), P(), P()),
        out_specs=(P(None, "gx", "gy", "gz"), P()),
        check_vma=False,
    )
```

```python
import jax
import jax.numpy as jnp
from jax import lax
from jax.experimental import pallas as pl
from jax.experimental.pallas import tpu as pltpu
from jax.sharding import PartitionSpec as P

ALL = ("gx", "gy", "gz")
CH = 32
LANES = 128


def shift_pair(up, down, axis):
    ends = lax.axis_size(axis) - 1
    from_prev = lax.ppermute(up, axis, [(i, i + 1) for i in range(ends)])
    from_next = lax.ppermute(down, axis, [(i + 1, i) for i in range(ends)])
    return from_prev, from_next


def roll(v, shift):
    return pltpu.roll(v, shift % LANES, 1)


def slot_of(row):
    return 8 * (row % 2) + row // 2


def gather_edges(tile, rows, load, lane):
    for row in rows:
        slot = slot_of(row)
        rolled = roll(load(row).astype(jnp.float32), 8 * slot + 4)
        tile = jnp.where(lane // 8 == slot, rolled, tile)
    return tile


def pack_mid_kernel(prev_ref, mine_ref, next_ref, tile_ref):
    lane = lax.broadcasted_iota(jnp.int32, (CH, LANES), 1)

    def layers(ref, base):
        def body(i, carry):
            tile = gather_edges(
                jnp.zeros((CH, LANES), jnp.float32), range(4, 12), lambda r: ref[i, r - 4], lane
            )
            tile_ref[base + i] = tile
            return carry

        lax.fori_loop(0, ref.shape[0], body, 0)

    layers(prev_ref, 0)
    layers(mine_ref, 7)
    layers(next_ref, 15)


def pack_mid(prev, mine, following):
    return pl.pallas_call(
        pack_mid_kernel,
        out_shape=jax.ShapeDtypeStruct((22, CH, LANES), jnp.float32),
        compiler_params=pltpu.CompilerParams(vmem_limit_bytes=16 << 20),
        cost_estimate=pl.CostEstimate(flops=0, bytes_accessed=1 << 21, transcendentals=0),
        name="pack_mid",
    )(prev, mine, following)


def pack_kernel(a1, b1, a2, b2, tile_ref, left_ref, right_ref, full):
    lane = lax.broadcasted_iota(jnp.int32, (CH, LANES), 1)
    low = (lane & 7) < 4

    def layers(above, below, base, count, skip):
        def body(i, carry):
            def load(r):
                return above[i + skip, r] if r < 4 else below[i + skip, r - 12]

            rows = list(range(4)) + list(range(12, 16))
            full[base + i] = gather_edges(tile_ref[base + i], rows, load, lane)
            return carry

        lax.fori_loop(0, count, body, 0)

    layers(a2, b2, 0, 7, 0)
    layers(a1, b1, 7, 8, 0)
    layers(a2, b2, 15, 7, 7)

    def group(g, carry):
        one, two = full[2 * g], full[2 * g + 1]
        right_ref[g] = jnp.where(low, one, roll(two, 4)).astype(jnp.bfloat16)
        left_ref[g] = jnp.where(low, roll(two, -4), one).astype(jnp.bfloat16)
        return carry

    lax.fori_loop(0, left_ref.shape[0], group, 0)


def pack_edges(a1, b1, a2, b2, tiles):
    out = jax.ShapeDtypeStruct((11, CH, LANES), jnp.bfloat16)
    return pl.pallas_call(
        pack_kernel,
        out_shape=(out, out),
        scratch_shapes=[pltpu.VMEM((22, CH, LANES), jnp.float32)],
        compiler_params=pltpu.CompilerParams(vmem_limit_bytes=16 << 20),
        cost_estimate=pl.CostEstimate(flops=0, bytes_accessed=1 << 21, transcendentals=0),
        name="pack_edges",
    )(a1, b1, a2, b2, tiles)


def convolve_layer(w, get, get_halo, m, pairs, put, put_halo):
    wide = lax.broadcasted_iota(jnp.int32, (2 * CH, LANES), 1)
    wide8 = wide & 7
    first = wide == 0
    n = 2 * CH

    def columns(p):
        if p < 0:
            return jnp.concatenate([get_halo(m + a) for a in range(3)], axis=0)
        return jnp.concatenate([get(m + a, 2 * p) for a in range(3)], axis=0)

    cross = None
    halo = None
    tiles = [-1] + list(pairs)
    for start in range(0, len(tiles), 2):
        here = tiles[start : start + 2]
        rhs = jnp.concatenate([columns(p) for p in here], axis=1)
        g = jnp.dot(w, rhs, preferred_element_type=jnp.float32)
        for k, p in enumerate(here):
            part = g[:, k * LANES : (k + 1) * LANES]
            before = roll(part[:n], 1)
            after = roll(part[2 * n :], -1)
            if p < 0:
                cross = jnp.where(wide8 == 4, before, after)
                halo = (
                    part[n : 2 * n]
                    + jnp.where(wide8 == 4, 0.0, before)
                    + jnp.where(wide8 == 3, 0.0, after)
                )
                continue
            mine = roll(cross, -(8 * p + 4))
            own = (
                part[n : 2 * n]
                + jnp.where(first, mine, before)
                + jnp.where(wide == LANES - 1, mine, after)
            )
            put(p, own)
            if put_halo is not None:
                give = roll(jnp.where(first, before, after), 8 * p + 4)
                halo = halo + jnp.where((wide == 8 * p + 3) | (wide == 8 * p + 4), give, 0.0)
    if put_halo is not None:
        put_halo(halo)


def store_halo(ref, m, v):
    for q, piece in enumerate((v[:CH], v[CH:], roll(v[:CH], -8), roll(v[CH:], -8))):
        ref[m, q * CH : (q + 1) * CH] = piece.astype(jnp.bfloat16)


def store(ref, m, p, v):
    ref[m, pl.ds(2 * p, 2)] = v.astype(jnp.bfloat16).reshape(2, CH, LANES)


def rows_of(ref):
    return lambda t, r: ref[t, pl.ds(r, 4)].reshape(4 * CH, LANES)


def first_kernel_body(
    prev, mine, following, a1, b1, a2, b2, rl_ref, rr_ref, w_ref,
    hid, hid_h, own_ref, own_h, slope_ref, slope_h, sum_ref,
    f_ref, edge, t_h, sems,
):
    moves = [
        (prev, f_ref.at[0:7, 4:12]),
        (mine, f_ref.at[7:15, 4:12]),
        (following, f_ref.at[15:22, 4:12]),
        (a1, f_ref.at[7:15, 0:4]),
        (b1, f_ref.at[7:15, 12:16]),
        (a2.at[0:7], f_ref.at[0:7, 0:4]),
        (a2.at[7:14], f_ref.at[15:22, 0:4]),
        (b2.at[0:7], f_ref.at[0:7, 12:16]),
        (b2.at[7:14], f_ref.at[15:22, 12:16]),
    ]
    copies = [pltpu.make_async_copy(x, y, sems.at[i]) for i, (x, y) in enumerate(moves)]
    for copy in copies:
        copy.start()

    lane = lax.broadcasted_iota(jnp.int32, (CH, LANES), 1)
    low = (lane & 7) < 4

    def unpack(g, carry):
        rl = rl_ref[g].astype(jnp.float32)
        rr = rr_ref[g].astype(jnp.float32)
        edge[2 * g] = jnp.where(low, rl, rr)
        edge[2 * g + 1] = jnp.where(low, roll(rl, -4), roll(rr, 4))
        return carry

    lax.fori_loop(0, rl_ref.shape[0], unpack, 0)

    def t_layer(t):
        return t + 2 + 4 * lax.shift_right_logical(t, 2)

    def s_layer(s):
        return s + 4 * lax.shift_right_logical(s + 2, 2)

    def t_halo(t, carry):
        tile = edge[t_layer(t)]
        for q, shift in enumerate((0, 64, -8, 56)):
            t_h[t, q * CH : (q + 1) * CH] = roll(tile, shift).astype(jnp.bfloat16)
        return carry

    lax.fori_loop(0, 12, t_halo, 0)
    for copy in copies:
        copy.wait()

    def slope_halo(i, row):
        tile = edge[i]
        q = row // 2
        return jnp.concatenate([roll(tile, 64 - 8 * q), roll(tile, -8 * (q + 1))], axis=0)

    def keep_slopes(m, carry):
        i = s_layer(m + 2)
        slope_ref[m] = f_ref[i, 3:13]
        slope_h[m] = slope_halo(i, 3)
        return carry

    lax.fori_loop(0, 6, keep_slopes, 0)

    def field_rows(t, r):
        return f_ref[t_layer(t), pl.ds(r, 4)].reshape(4 * CH, LANES)

    def stage_hidden(m, carry):
        i = s_layer(m)

        def put(p, v):
            slope = f_ref[i, pl.ds(2 * p + 1, 2)].reshape(2 * CH, LANES)
            store(hid, m, p, slope.astype(jnp.float32) * v)

        def put_halo(v):
            store_halo(hid_h, m, slope_halo(i, 1) * v)

        convolve_layer(w_ref[0], field_rows, lambda t: t_h[t], m, range(7), put, put_halo)
        return carry

    lax.fori_loop(0, 10, stage_hidden, 0)
    sum_ref[...] = jnp.zeros_like(sum_ref)

    def stage_own(m, carry):
        def put(p, v):
            own_ref[m, pl.ds(2 * p - 2, 2)] = v.astype(jnp.bfloat16).reshape(2, CH, LANES)
            square = v * v
            part = square[0:8]
            for q in range(1, 8):
                part = part + square[8 * q : 8 * q + 8]
            sum_ref[...] += part

        def put_halo(v):
            own_h[m] = v

        convolve_layer(
            w_ref[1], rows_of(hid), lambda t: hid_h[t], m + 2, range(1, 5), put, put_halo
        )
        return carry

    lax.fori_loop(0, 4, stage_own, 0)


def first_convs(pieces, rl, rr, weights):
    shape = jax.ShapeDtypeStruct
    return pl.pallas_call(
        first_kernel_body,
        out_shape=(
            shape((10, 14, CH, LANES), jnp.bfloat16),
            shape((10, 4 * CH, LANES), jnp.bfloat16),
            shape((4, 8, CH, LANES), jnp.bfloat16),
            shape((4, 2 * CH, LANES), jnp.float32),
            shape((6, 10, CH, LANES), jnp.bfloat16),
            shape((6, 2 * CH, LANES), jnp.float32),
            shape((8, LANES), jnp.float32),
        ),
        in_specs=[pl.BlockSpec(memory_space=pl.ANY)] * 7
        + [pl.BlockSpec(memory_space=pltpu.VMEM)] * 3,
        scratch_shapes=[
            pltpu.VMEM((22, 16, CH, LANES), jnp.bfloat16),
            pltpu.VMEM((22, CH, LANES), jnp.float32),
            pltpu.VMEM((12, 4 * CH, LANES), jnp.bfloat16),
            pltpu.SemaphoreType.DMA((9,)),
        ],
        compiler_params=pltpu.CompilerParams(vmem_limit_bytes=16 << 20),
        cost_estimate=pl.CostEstimate(flops=8 << 30, bytes_accessed=8 << 20, transcendentals=0),
        name="first_convs",
    )(*pieces, rl, rr, weights)


def second_kernel_body(
    place, hid, hid_h, own_ref, own_h, slope_ref, slope_h, w_ref, out_ref, img, img_h, pul, pul_h
):
    wide = lax.broadcasted_iota(jnp.int32, (2 * CH, LANES), 1)
    wide8 = wide & 7
    gx, gy, gz = place[0], place[1], place[2]
    nx, ny, nz = place[3], place[4], place[5]
    top_in = jnp.where(gy > 0, 1.0, 0.0)
    low_in = jnp.where(gy < ny, 1.0, 0.0)
    halo_in = jnp.where(wide8 < 4, jnp.where(gz > 0, 1.0, 0.0), jnp.where(gz < nz, 1.0, 0.0))
    halo_in = jnp.where(wide < 8, halo_in * top_in, halo_in)
    halo_in = jnp.where(wide >= 40, halo_in * low_in, halo_in)

    def image_layer(m, x_in, pairs, merge):
        def put(p, v):
            keep = x_in * (top_in if p == 0 else low_in if p == 5 else 1.0)
            store(img, m, p, v * keep)

        def put_halo(v):
            store_halo(img_h, m, merge(v) * (halo_in * x_in))

        convolve_layer(w_ref[0], rows_of(hid), lambda t: hid_h[t], m, pairs, put, put_halo)

    def stage_ends(i, carry):
        m = jnp.where(i < 2, i, i + 4)
        x_in = jnp.where(((i >= 2) | (gx > 0)) & ((i < 2) | (gx < nx)), 1.0, 0.0)
        image_layer(m, x_in, range(6), lambda v: v)
        return carry

    lax.fori_loop(0, 4, stage_ends, 0)

    def stage_rim(i, carry):
        m = i + 2
        img[m, 2:10] = own_ref[i]
        outer = (wide < 8) | (wide >= 40)
        image_layer(m, 1.0, (0, 5), lambda v: jnp.where(outer, v, own_h[i]))
        return carry

    lax.fori_loop(0, 4, stage_rim, 0)

    def stage_pulled(m, carry):
        def put(p, v):
            slope = slope_ref[m, pl.ds(2 * p, 2)].reshape(2 * CH, LANES)
            store(pul, m, p, slope.astype(jnp.float32) * v)

        def put_halo(v):
            store_halo(pul_h, m, slope_h[m] * v)

        convolve_layer(w_ref[1], rows_of(img), lambda t: img_h[t], m, range(5), put, put_halo)
        return carry

    lax.fori_loop(0, 6, stage_pulled, 0)

    def stage_out(m, carry):
        def put(p, v):
            out_ref[m, pl.ds(2 * p, 2)] = v.reshape(2, CH, LANES)

        convolve_layer(w_ref[2], rows_of(pul), lambda t: pul_h[t], m, range(4), put, None)
        return carry

    lax.fori_loop(0, 4, stage_out, 0)


def second_convs(place, fields, weights):
    return pl.pallas_call(
        second_kernel_body,
        out_shape=jax.ShapeDtypeStruct((4, 8, CH, LANES), jnp.float32),
        in_specs=[pl.BlockSpec(memory_space=pltpu.SMEM)]
        + [pl.BlockSpec(memory_space=pltpu.VMEM)] * 7,
        scratch_shapes=[
            pltpu.VMEM((8, 12, CH, LANES), jnp.bfloat16),
            pltpu.VMEM((8, 4 * CH, LANES), jnp.bfloat16),
            pltpu.VMEM((6, 10, CH, LANES), jnp.bfloat16),
            pltpu.VMEM((6, 4 * CH, LANES), jnp.bfloat16),
        ],
        compiler_params=pltpu.CompilerParams(vmem_limit_bytes=16 << 20),
        cost_estimate=pl.CostEstimate(flops=8 << 30, bytes_accessed=4 << 20, transcendentals=0),
        name="second_convs",
    )(place, *fields, weights)


def pair_matrix(kernel):
    taps = kernel.reshape(3, 3, 3, CH, CH)
    none = ((0, 0), (0, 0), (0, 0), (0, 0))
    top = jnp.pad(taps, (none[0], (0, 1)) + none[:3])
    low = jnp.pad(taps, (none[0], (1, 0)) + none[:3])
    both = jnp.stack([top, low])
    return both.transpose(3, 0, 4, 1, 2, 5).reshape(6 * CH, 12 * CH)


def on_device(tangent, slopes, first_kernel, second_kernel):
    t = tangent.transpose(1, 2, 0, 3)
    s = slopes.transpose(1, 2, 0, 3)
    mine = jnp.concatenate([s[0:3], t, s[3:4]], axis=0)
    prev, following = shift_pair(mine[1:8], mine[0:7], "gx")
    a1, b1 = shift_pair(mine[:, 4:8], mine[:, 0:4], "gy")
    to_below = jnp.concatenate([prev[:, 4:8], following[:, 4:8]], axis=0)
    to_above = jnp.concatenate([prev[:, 0:4], following[:, 0:4]], axis=0)
    a2, b2 = shift_pair(to_below, to_above, "gy")
    tiles = pack_mid(prev, mine, following)
    left_edge, right_edge = pack_edges(a1, b1, a2, b2, tiles)
    rl, rr = shift_pair(right_edge, left_edge, "gz")

    adjoint = lambda k: k[::-1].transpose(0, 2, 1)
    second = pair_matrix(second_kernel)
    forward = jnp.stack([pair_matrix(first_kernel), second])
    backward = jnp.stack(
        [second, pair_matrix(adjoint(second_kernel)), pair_matrix(adjoint(first_kernel))]
    )
    place = jnp.stack(
        [lax.axis_index(a) for a in ALL] + [jnp.int32(lax.axis_size(a) - 1) for a in ALL]
    ).astype(jnp.int32)
    *fields, squares = first_convs((prev, mine, following, a1, b1, a2, b2), rl, rr, forward)

    def exchange(part, axes):
        count = lax.axis_size(axes)
        spread = jnp.broadcast_to(part, (count, LANES))
        return jnp.sum(lax.all_to_all(spread, axes, 0, 0, tiled=True), axis=0, keepdims=True)

    part = exchange(jnp.sum(squares, axis=0, keepdims=True), ("gy", "gz"))
    part, *fields = lax.optimization_barrier((part, *fields))
    result = second_convs(place, fields, backward)
    part = exchange(part, "gx")
    jvp_norm = jnp.sqrt(jnp.sum(part) + 1e-06)
    next_vector = result.transpose(2, 0, 1, 3) / jvp_norm
    return (next_vector, jvp_norm.reshape(1))


def solution(mesh):
    return jax.shard_map(
        on_device,
        mesh=mesh,
        in_specs=(P(None, "gx", "gy", "gz"), P(None, "gx", "gy", "gz"), P(), P()),
        out_specs=(P(None, "gx", "gy", "gz"), P()),
        check_vma=False,
    )
```

```python
import jax
import jax.numpy as jnp
from jax import lax
from jax.experimental import pallas as pl
from jax.experimental.pallas import tpu as pltpu
from jax.sharding import PartitionSpec as P

ALL = ("gx", "gy", "gz")
CH = 32
LANES = 128


def shift_pair(up, down, axis):
    ends = lax.axis_size(axis) - 1
    from_prev = lax.ppermute(up, axis, [(i, i + 1) for i in range(ends)])
    from_next = lax.ppermute(down, axis, [(i + 1, i) for i in range(ends)])
    return from_prev, from_next


def roll(v, shift):
    return pltpu.roll(v, shift % LANES, 1)


def slot_of(row):
    return 8 * (row % 2) + row // 2


def gather_edges(tile, rows, load, lane):
    for row in rows:
        slot = slot_of(row)
        rolled = roll(load(row).astype(jnp.float32), 8 * slot + 4)
        tile = jnp.where(lane // 8 == slot, rolled, tile)
    return tile


def rows_kernel(prev_ref, next_ref, low_ref, top_ref):
    low_ref[0:7] = prev_ref[:, 4:8]
    low_ref[7:14] = next_ref[:, 4:8]
    top_ref[0:7] = prev_ref[:, 0:4]
    top_ref[7:14] = next_ref[:, 0:4]


def edge_rows(prev, following):
    out = jax.ShapeDtypeStruct((14, 4, CH, LANES), jnp.bfloat16)
    return pl.pallas_call(
        rows_kernel,
        out_shape=(out, out),
        compiler_params=pltpu.CompilerParams(vmem_limit_bytes=16 << 20),
        cost_estimate=pl.CostEstimate(flops=0, bytes_accessed=1 << 21, transcendentals=0),
        name="edge_rows",
    )(prev, following)


OUTER = list(range(4)) + list(range(12, 16))


def pack_mid_kernel(prev_ref, mine_ref, next_ref, a1, b1, tile_ref):
    lane = lax.broadcasted_iota(jnp.int32, (CH, LANES), 1)
    none = jnp.zeros((CH, LANES), jnp.float32)

    def layers(ref, base):
        def body(i, carry):
            tile_ref[base + i] = gather_edges(none, range(4, 12), lambda r: ref[i, r - 4], lane)
            return carry

        lax.fori_loop(0, ref.shape[0], body, 0)

    def own(i, carry):
        def load(r):
            if 4 <= r < 12:
                return mine_ref[i, r - 4]
            return a1[i, r] if r < 4 else b1[i, r - 12]

        tile_ref[7 + i] = gather_edges(none, range(16), load, lane)
        return carry

    layers(prev_ref, 0)
    lax.fori_loop(0, 8, own, 0)
    layers(next_ref, 15)


def pack_mid(prev, mine, following, a1, b1):
    return pl.pallas_call(
        pack_mid_kernel,
        out_shape=jax.ShapeDtypeStruct((22, CH, LANES), jnp.float32),
        compiler_params=pltpu.CompilerParams(vmem_limit_bytes=16 << 20),
        cost_estimate=pl.CostEstimate(flops=0, bytes_accessed=1 << 21, transcendentals=0),
        name="pack_mid",
    )(prev, mine, following, a1, b1)


def pack_kernel(a2, b2, tile_ref, left_ref, right_ref, full):
    lane = lax.broadcasted_iota(jnp.int32, (CH, LANES), 1)
    low = (lane & 7) < 4
    full[7:15] = tile_ref[7:15]

    def received(i, carry):
        at = jnp.where(i < 7, i, i + 8)
        load = lambda r: a2[i, r] if r < 4 else b2[i, r - 12]
        full[at] = gather_edges(tile_ref[at], OUTER, load, lane)
        return carry

    lax.fori_loop(0, 14, received, 0)

    def group(g, carry):
        one, two = full[2 * g], full[2 * g + 1]
        right_ref[g] = jnp.where(low, one, roll(two, 4)).astype(jnp.bfloat16)
        left_ref[g] = jnp.where(low, roll(two, -4), one).astype(jnp.bfloat16)
        return carry

    lax.fori_loop(0, left_ref.shape[0], group, 0)


def pack_edges(a2, b2, tiles):
    out = jax.ShapeDtypeStruct((11, CH, LANES), jnp.bfloat16)
    return pl.pallas_call(
        pack_kernel,
        out_shape=(out, out),
        scratch_shapes=[pltpu.VMEM((22, CH, LANES), jnp.float32)],
        compiler_params=pltpu.CompilerParams(vmem_limit_bytes=16 << 20),
        cost_estimate=pl.CostEstimate(flops=0, bytes_accessed=1 << 21, transcendentals=0),
        name="pack_edges",
    )(a2, b2, tiles)


def convolve_layer(w, get, get_halo, m, pairs, put, put_halo):
    wide = lax.broadcasted_iota(jnp.int32, (2 * CH, LANES), 1)
    wide8 = wide & 7
    first = wide == 0
    n = 2 * CH

    def columns(p):
        if p < 0:
            return jnp.concatenate([get_halo(m + a) for a in range(3)], axis=0)
        return jnp.concatenate([get(m + a, 2 * p) for a in range(3)], axis=0)

    cross = None
    halo = None
    tiles = [-1] + list(pairs)
    for start in range(0, len(tiles), 2):
        here = tiles[start : start + 2]
        rhs = jnp.concatenate([columns(p) for p in here], axis=1)
        g = jnp.dot(w, rhs, preferred_element_type=jnp.float32)
        for k, p in enumerate(here):
            part = g[:, k * LANES : (k + 1) * LANES]
            before = roll(part[:n], 1)
            after = roll(part[2 * n :], -1)
            if p < 0:
                cross = jnp.where(wide8 == 4, before, after)
                halo = (
                    part[n : 2 * n]
                    + jnp.where(wide8 == 4, 0.0, before)
                    + jnp.where(wide8 == 3, 0.0, after)
                )
                continue
            mine = roll(cross, -(8 * p + 4))
            own = (
                part[n : 2 * n]
                + jnp.where(first, mine, before)
                + jnp.where(wide == LANES - 1, mine, after)
            )
            put(p, own)
            if put_halo is not None:
                give = roll(jnp.where(first, before, after), 8 * p + 4)
                halo = halo + jnp.where((wide == 8 * p + 3) | (wide == 8 * p + 4), give, 0.0)
    if put_halo is not None:
        put_halo(halo)


def store_halo(ref, m, v):
    for q, piece in enumerate((v[:CH], v[CH:], roll(v[:CH], -8), roll(v[CH:], -8))):
        ref[m, q * CH : (q + 1) * CH] = piece.astype(jnp.bfloat16)


def store(ref, m, p, v):
    ref[m, pl.ds(2 * p, 2)] = v.astype(jnp.bfloat16).reshape(2, CH, LANES)


def rows_of(ref):
    return lambda t, r: ref[t, pl.ds(r, 4)].reshape(4 * CH, LANES)


def first_kernel_body(
    prev, mine, following, a1, b1, a2, b2, rl_ref, rr_ref, w_ref,
    hid_out, hid_h_out, own_out, own_h_out, slope_out, slope_h_out, sum_ref,
    f_ref, edge, t_h, hid, hid_h, own_ref, own_h, slope_h, sum_acc, sems, out_sems,
):
    moves = [
        (prev, f_ref.at[0:7, 4:12]),
        (mine, f_ref.at[7:15, 4:12]),
        (following, f_ref.at[15:22, 4:12]),
        (a1, f_ref.at[7:15, 0:4]),
        (b1, f_ref.at[7:15, 12:16]),
        (a2.at[0:7], f_ref.at[0:7, 0:4]),
        (a2.at[7:14], f_ref.at[15:22, 0:4]),
        (b2.at[0:7], f_ref.at[0:7, 12:16]),
        (b2.at[7:14], f_ref.at[15:22, 12:16]),
    ]
    copies = [pltpu.make_async_copy(x, y, sems.at[i]) for i, (x, y) in enumerate(moves)]
    for copy in copies:
        copy.start()

    lane = lax.broadcasted_iota(jnp.int32, (CH, LANES), 1)
    low = (lane & 7) < 4

    def unpack(g, carry):
        rl = rl_ref[g].astype(jnp.float32)
        rr = rr_ref[g].astype(jnp.float32)
        edge[2 * g] = jnp.where(low, rl, rr)
        edge[2 * g + 1] = jnp.where(low, roll(rl, -4), roll(rr, 4))
        return carry

    lax.fori_loop(0, rl_ref.shape[0], unpack, 0)

    def t_layer(t):
        return t + 2 + 4 * lax.shift_right_logical(t, 2)

    def s_layer(s):
        return s + 4 * lax.shift_right_logical(s + 2, 2)

    def t_halo(t, carry):
        tile = edge[t_layer(t)]
        for q, shift in enumerate((0, 64, -8, 56)):
            t_h[t, q * CH : (q + 1) * CH] = roll(tile, shift).astype(jnp.bfloat16)
        return carry

    lax.fori_loop(0, 12, t_halo, 0)

    def slope_halo(m, row):
        tile = edge[s_layer(m)]
        q = row // 2
        return jnp.concatenate([roll(tile, 64 - 8 * q), roll(tile, -8 * (q + 1))], axis=0)

    def keep_slopes(m, carry):
        slope_h[m] = slope_halo(m + 2, 3)
        return carry

    def field_rows(t, r):
        return f_ref[t_layer(t), pl.ds(r, 4)].reshape(4 * CH, LANES)

    lax.fori_loop(0, 6, keep_slopes, 0)
    for copy in copies:
        copy.wait()

    def stage_hidden(m, carry):
        def put(p, v):
            slope = f_ref[s_layer(m), pl.ds(2 * p + 1, 2)].reshape(2 * CH, LANES)
            store(hid, m, p, slope.astype(jnp.float32) * v)

        def put_halo(v):
            store_halo(hid_h, m, slope_halo(m, 1) * v)

        convolve_layer(w_ref[0], field_rows, lambda t: t_h[t], m, range(7), put, put_halo)
        return carry

    lax.fori_loop(0, 10, stage_hidden, 0)
    early = [
        (hid, hid_out), (hid_h, hid_h_out), (slope_h, slope_h_out),
        (f_ref.at[6:10, 3:13], slope_out.at[0:4]), (f_ref.at[14:16, 3:13], slope_out.at[4:6]),
    ]
    late = [(own_ref, own_out), (own_h, own_h_out)]
    writes = [pltpu.make_async_copy(x, y, out_sems.at[i]) for i, (x, y) in enumerate(early + late)]
    for copy in writes[:5]:
        copy.start()
    sum_acc[...] = jnp.zeros_like(sum_acc)

    def stage_own(m, carry):
        def put(p, v):
            own_ref[m, pl.ds(2 * p - 2, 2)] = v.astype(jnp.bfloat16).reshape(2, CH, LANES)
            square = v * v
            part = square[0:8]
            for q in range(1, 8):
                part = part + square[8 * q : 8 * q + 8]
            sum_acc[...] += part

        def put_halo(v):
            own_h[m] = v

        convolve_layer(
            w_ref[1], rows_of(hid), lambda t: hid_h[t], m + 2, range(1, 5), put, put_halo
        )
        return carry

    lax.fori_loop(0, 4, stage_own, 0)
    for copy in writes[5:]:
        copy.start()
    total = jnp.sum(sum_acc[...], axis=0, keepdims=True)
    for i in range(sum_ref.shape[0]):
        sum_ref[i] = total
    for copy in writes:
        copy.wait()


def first_convs(pieces, rl, rr, weights, spread):
    shape = jax.ShapeDtypeStruct
    anywhere = pl.BlockSpec(memory_space=pl.ANY)
    local = pl.BlockSpec(memory_space=pltpu.VMEM)
    fields = (
        shape((10, 14, CH, LANES), jnp.bfloat16),
        shape((10, 4 * CH, LANES), jnp.bfloat16),
        shape((4, 8, CH, LANES), jnp.bfloat16),
        shape((4, 2 * CH, LANES), jnp.float32),
        shape((6, 10, CH, LANES), jnp.bfloat16),
        shape((6, 2 * CH, LANES), jnp.float32),
    )
    keep = [pltpu.VMEM(fields[i].shape, fields[i].dtype) for i in (0, 1, 2, 3, 5)]
    return pl.pallas_call(
        first_kernel_body,
        out_shape=(*fields, shape((spread, 1, LANES), jnp.float32)),
        in_specs=[anywhere] * 7 + [local] * 3,
        out_specs=(*([anywhere] * 6), local),
        scratch_shapes=[
            pltpu.VMEM((22, 16, CH, LANES), jnp.bfloat16),
            pltpu.VMEM((22, CH, LANES), jnp.float32),
            pltpu.VMEM((12, 4 * CH, LANES), jnp.bfloat16),
            *keep,
            pltpu.VMEM((8, LANES), jnp.float32),
            pltpu.SemaphoreType.DMA((9,)),
            pltpu.SemaphoreType.DMA((7,)),
        ],
        compiler_params=pltpu.CompilerParams(vmem_limit_bytes=62 << 20),
        cost_estimate=pl.CostEstimate(flops=8 << 30, bytes_accessed=8 << 20, transcendentals=0),
        name="first_convs",
    )(*pieces, rl, rr, weights)


def second_kernel_body(
    place, hid_in, hid_h_in, own_in, own_h_in, slope_in, slope_h_in, w_ref, after, out_ref,
    hid, hid_h, own_h, slope_ref, slope_h, img, img_h, pul, pul_h, sems,
):
    moves = [
        (hid_in, hid), (hid_h_in, hid_h), (own_in, img.at[2:6, 2:10]), (own_h_in, own_h),
        (slope_in, slope_ref), (slope_h_in, slope_h),
    ]
    copies = [pltpu.make_async_copy(x, y, sems.at[i]) for i, (x, y) in enumerate(moves)]
    for copy in copies:
        copy.start()
    for copy in copies[:2]:
        copy.wait()
    wide = lax.broadcasted_iota(jnp.int32, (2 * CH, LANES), 1)
    wide8 = wide & 7
    gx, gy, gz = place[0], place[1], place[2]
    nx, ny, nz = place[3], place[4], place[5]
    top_in = jnp.where(gy > 0, 1.0, 0.0)
    low_in = jnp.where(gy < ny, 1.0, 0.0)
    halo_in = jnp.where(wide8 < 4, jnp.where(gz > 0, 1.0, 0.0), jnp.where(gz < nz, 1.0, 0.0))
    halo_in = jnp.where(wide < 8, halo_in * top_in, halo_in)
    halo_in = jnp.where(wide >= 40, halo_in * low_in, halo_in)

    def image_layer(m, x_in, pairs, merge):
        def put(p, v):
            keep = x_in * (top_in if p == 0 else low_in if p == 5 else 1.0)
            store(img, m, p, v * keep)

        def put_halo(v):
            store_halo(img_h, m, merge(v) * (halo_in * x_in))

        convolve_layer(w_ref[1], rows_of(hid), lambda t: hid_h[t], m, pairs, put, put_halo)

    def stage_ends(i, carry):
        m = jnp.where(i < 2, i, i + 4)
        x_in = jnp.where(((i >= 2) | (gx > 0)) & ((i < 2) | (gx < nx)), 1.0, 0.0)
        image_layer(m, x_in, range(6), lambda v: v)
        return carry

    lax.fori_loop(0, 4, stage_ends, 0)

    for copy in copies[2:]:
        copy.wait()

    def stage_rim(i, carry):
        m = i + 2
        outer = (wide < 8) | (wide >= 40)
        image_layer(m, 1.0, (0, 5), lambda v: jnp.where(outer, v, own_h[i]))
        return carry

    lax.fori_loop(0, 4, stage_rim, 0)

    def stage_pulled(m, carry):
        def put(p, v):
            slope = slope_ref[m, pl.ds(2 * p, 2)].reshape(2 * CH, LANES)
            store(pul, m, p, slope.astype(jnp.float32) * v)

        def put_halo(v):
            store_halo(pul_h, m, slope_h[m] * v)

        convolve_layer(w_ref[2], rows_of(img), lambda t: img_h[t], m, range(5), put, put_halo)
        return carry

    lax.fori_loop(0, 6, stage_pulled, 0)

    def stage_out(m, carry):
        def put(p, v):
            out_ref[m, pl.ds(2 * p, 2)] = v.reshape(2, CH, LANES)

        convolve_layer(w_ref[3], rows_of(pul), lambda t: pul_h[t], m, range(4), put, None)
        return carry

    lax.fori_loop(0, 4, stage_out, 0)


def second_convs(place, fields, weights, after):
    return pl.pallas_call(
        second_kernel_body,
        out_shape=jax.ShapeDtypeStruct((4, 8, CH, LANES), jnp.float32),
        in_specs=[pl.BlockSpec(memory_space=pltpu.SMEM)]
        + [pl.BlockSpec(memory_space=pl.ANY)] * 6
        + [pl.BlockSpec(memory_space=pltpu.VMEM)] * 2,
        scratch_shapes=[
            *[pltpu.VMEM(f.shape, f.dtype) for i, f in enumerate(fields) if i != 2],
            pltpu.VMEM((8, 12, CH, LANES), jnp.bfloat16),
            pltpu.VMEM((8, 4 * CH, LANES), jnp.bfloat16),
            pltpu.VMEM((6, 10, CH, LANES), jnp.bfloat16),
            pltpu.VMEM((6, 4 * CH, LANES), jnp.bfloat16),
            pltpu.SemaphoreType.DMA((6,)),
        ],
        compiler_params=pltpu.CompilerParams(vmem_limit_bytes=62 << 20),
        cost_estimate=pl.CostEstimate(flops=8 << 30, bytes_accessed=4 << 20, transcendentals=0),
        name="second_convs",
    )(place, *fields, weights, after)


def weights_kernel(k1_ref, k2_ref, w_ref):
    w_ref[...] = jnp.zeros_like(w_ref)
    for which, (ref, adjoint) in enumerate(
        ((k1_ref, False), (k2_ref, False), (k2_ref, True), (k1_ref, True))
    ):
        for tap in range(27):
            a, b, c = tap // 9, tap // 3 % 3, tap % 3
            if adjoint:
                block = ref[26 - tap].astype(jnp.float32).T.astype(jnp.bfloat16)
            else:
                block = ref[tap]
            for row in range(2):
                top = (2 * c + row) * CH
                left = (4 * a + b + row) * CH
                w_ref[which, top : top + CH, left : left + CH] = block


def pair_matrices(first_kernel, second_kernel):
    return pl.pallas_call(
        weights_kernel,
        out_shape=jax.ShapeDtypeStruct((4, 6 * CH, 12 * CH), jnp.bfloat16),
        compiler_params=pltpu.CompilerParams(vmem_limit_bytes=8 << 20),
        cost_estimate=pl.CostEstimate(flops=0, bytes_accessed=4 << 20, transcendentals=0),
        name="pair_matrices",
    )(first_kernel, second_kernel)


def on_device(tangent, slopes, first_kernel, second_kernel):
    t = tangent.transpose(1, 2, 0, 3)
    s = slopes.transpose(1, 2, 0, 3)
    mine = jnp.concatenate([s[0:3], t, s[3:4]], axis=0)
    prev, following = shift_pair(mine[1:8], mine[0:7], "gx")
    a1, b1 = shift_pair(mine[:, 4:8], mine[:, 0:4], "gy")
    prev, following, a1, b1 = lax.optimization_barrier((prev, following, a1, b1))
    low, top = edge_rows(prev, following)
    a2, b2 = shift_pair(low, top, "gy")
    weights = pair_matrices(first_kernel, second_kernel)
    left_edge, right_edge = pack_edges(a2, b2, pack_mid(prev, mine, following, a1, b1))
    rl, rr = shift_pair(right_edge, left_edge, "gz")
    plane = lax.axis_size(("gy", "gz"))
    pieces = (prev, mine, following, a1, b1, a2, b2)
    *fields, spread = first_convs(pieces, rl, rr, weights, plane)

    def collect(v, axes):
        return jnp.sum(lax.all_to_all(v, axes, 0, 0, tiled=True), axis=0, keepdims=True)

    place = jnp.stack(
        [lax.axis_index(a) for a in ALL] + [jnp.int32(lax.axis_size(a) - 1) for a in ALL]
    ).astype(jnp.int32)
    part = collect(spread, ("gy", "gz"))
    result = second_convs(place, fields, weights, part)
    count = lax.axis_size("gx")
    part = collect(jnp.broadcast_to(part, (count, 1, LANES)), "gx")
    jvp_norm = jnp.sqrt(jnp.sum(part) + 1e-06)
    next_vector = result.transpose(2, 0, 1, 3) / jvp_norm
    return (next_vector, jvp_norm.reshape(1))


def solution(mesh):
    return jax.shard_map(
        on_device,
        mesh=mesh,
        in_specs=(P(None, "gx", "gy", "gz"), P(None, "gx", "gy", "gz"), P(), P()),
        out_specs=(P(None, "gx", "gy", "gz"), P()),
        check_vma=False,
    )
```

```python
import jax
import jax.numpy as jnp
from jax import lax
from jax.experimental import pallas as pl
from jax.experimental.pallas import tpu as pltpu
from jax.sharding import PartitionSpec as P

ALL = ("gx", "gy", "gz")
CH = 32
LANES = 128


def shift_pair(up, down, axis):
    ends = lax.axis_size(axis) - 1
    from_prev = lax.ppermute(up, axis, [(i, i + 1) for i in range(ends)])
    from_next = lax.ppermute(down, axis, [(i + 1, i) for i in range(ends)])
    return from_prev, from_next


def roll(v, shift):
    return pltpu.roll(v, shift % LANES, 1)


def slot_of(row):
    return 8 * (row % 2) + row // 2


def gather_edges(tile, rows, load, lane):
    for row in rows:
        slot = slot_of(row)
        rolled = roll(load(row).astype(jnp.float32), 8 * slot + 4)
        tile = jnp.where(lane // 8 == slot, rolled, tile)
    return tile


def rows_kernel(prev_ref, next_ref, low_ref, top_ref):
    low_ref[0:7] = prev_ref[:, 4:8]
    low_ref[7:14] = next_ref[:, 4:8]
    top_ref[0:7] = prev_ref[:, 0:4]
    top_ref[7:14] = next_ref[:, 0:4]


def edge_rows(prev, following):
    out = jax.ShapeDtypeStruct((14, 4, CH, LANES), jnp.bfloat16)
    return pl.pallas_call(
        rows_kernel,
        out_shape=(out, out),
        compiler_params=pltpu.CompilerParams(vmem_limit_bytes=16 << 20),
        cost_estimate=pl.CostEstimate(flops=0, bytes_accessed=1 << 21, transcendentals=0),
        name="edge_rows",
    )(prev, following)


OUTER = list(range(4)) + list(range(12, 16))


def pack_mid_kernel(prev_ref, mine_ref, next_ref, a1, b1, tile_ref):
    lane = lax.broadcasted_iota(jnp.int32, (CH, LANES), 1)
    none = jnp.zeros((CH, LANES), jnp.float32)

    def layers(ref, base):
        def body(i, carry):
            tile_ref[base + i] = gather_edges(none, range(4, 12), lambda r: ref[i, r - 4], lane)
            return carry

        lax.fori_loop(0, ref.shape[0], body, 0)

    def own(i, carry):
        def load(r):
            if 4 <= r < 12:
                return mine_ref[i, r - 4]
            return a1[i, r] if r < 4 else b1[i, r - 12]

        tile_ref[7 + i] = gather_edges(none, range(16), load, lane)
        return carry

    layers(prev_ref, 0)
    lax.fori_loop(0, 8, own, 0)
    layers(next_ref, 15)


def pack_mid(prev, mine, following, a1, b1):
    return pl.pallas_call(
        pack_mid_kernel,
        out_shape=jax.ShapeDtypeStruct((22, CH, LANES), jnp.float32),
        compiler_params=pltpu.CompilerParams(vmem_limit_bytes=16 << 20),
        cost_estimate=pl.CostEstimate(flops=0, bytes_accessed=1 << 21, transcendentals=0),
        name="pack_mid",
    )(prev, mine, following, a1, b1)


def pack_kernel(a2, b2, tile_ref, left_ref, right_ref, full):
    lane = lax.broadcasted_iota(jnp.int32, (CH, LANES), 1)
    low = (lane & 7) < 4
    full[7:15] = tile_ref[7:15]

    def received(i, carry):
        at = jnp.where(i < 7, i, i + 8)
        load = lambda r: a2[i, r] if r < 4 else b2[i, r - 12]
        full[at] = gather_edges(tile_ref[at], OUTER, load, lane)
        return carry

    lax.fori_loop(0, 14, received, 0)

    def group(g, carry):
        one, two = full[2 * g], full[2 * g + 1]
        right_ref[g] = jnp.where(low, one, roll(two, 4)).astype(jnp.bfloat16)
        left_ref[g] = jnp.where(low, roll(two, -4), one).astype(jnp.bfloat16)
        return carry

    lax.fori_loop(0, left_ref.shape[0], group, 0)


def pack_edges(a2, b2, tiles):
    out = jax.ShapeDtypeStruct((11, CH, LANES), jnp.bfloat16)
    return pl.pallas_call(
        pack_kernel,
        out_shape=(out, out),
        scratch_shapes=[pltpu.VMEM((22, CH, LANES), jnp.float32)],
        compiler_params=pltpu.CompilerParams(vmem_limit_bytes=16 << 20),
        cost_estimate=pl.CostEstimate(flops=0, bytes_accessed=1 << 21, transcendentals=0),
        name="pack_edges",
    )(a2, b2, tiles)


def convolve_layer(w, get, get_halo, m, pairs, put, put_halo):
    wide = lax.broadcasted_iota(jnp.int32, (2 * CH, LANES), 1)
    wide8 = wide & 7
    first = wide == 0
    n = 2 * CH

    def columns(p):
        if p < 0:
            return jnp.concatenate([get_halo(m + a) for a in range(3)], axis=0)
        return jnp.concatenate([get(m + a, 2 * p) for a in range(3)], axis=0)

    cross = None
    halo = None
    tiles = [-1] + list(pairs)
    for start in range(0, len(tiles), 2):
        here = tiles[start : start + 2]
        rhs = jnp.concatenate([columns(p) for p in here], axis=1)
        g = jnp.dot(w, rhs, preferred_element_type=jnp.float32)
        for k, p in enumerate(here):
            part = g[:, k * LANES : (k + 1) * LANES]
            before = roll(part[:n], 1)
            after = roll(part[2 * n :], -1)
            if p < 0:
                cross = jnp.where(wide8 == 4, before, after)
                halo = (
                    part[n : 2 * n]
                    + jnp.where(wide8 == 4, 0.0, before)
                    + jnp.where(wide8 == 3, 0.0, after)
                )
                continue
            mine = roll(cross, -(8 * p + 4))
            own = (
                part[n : 2 * n]
                + jnp.where(first, mine, before)
                + jnp.where(wide == LANES - 1, mine, after)
            )
            put(p, own)
            if put_halo is not None:
                give = roll(jnp.where(first, before, after), 8 * p + 4)
                halo = halo + jnp.where((wide == 8 * p + 3) | (wide == 8 * p + 4), give, 0.0)
    if put_halo is not None:
        put_halo(halo)


def store_halo(ref, m, v):
    for q, piece in enumerate((v[:CH], v[CH:], roll(v[:CH], -8), roll(v[CH:], -8))):
        ref[m, q * CH : (q + 1) * CH] = piece.astype(jnp.bfloat16)


def store(ref, m, p, v):
    ref[m, pl.ds(2 * p, 2)] = v.astype(jnp.bfloat16).reshape(2, CH, LANES)


def rows_of(ref):
    return lambda t, r: ref[t, pl.ds(r, 4)].reshape(4 * CH, LANES)


def first_kernel_body(
    prev, mine, following, a1, b1, a2, b2, rl_in, rr_in, w_in,
    hid_out, hid_h_out, own_out, own_h_out, slope_out, slope_h_out, sum_ref,
    f_ref, rl_ref, rr_ref, w_ref, edge, t_h, hid, hid_h, own_ref, own_h, slope_h, sum_acc, sems, out_sems,
):
    moves = [
        (rl_in, rl_ref),
        (rr_in, rr_ref),
        (w_in.at[0:2], w_ref),
        (prev, f_ref.at[0:7, 4:12]),
        (a2.at[0:7], f_ref.at[0:7, 0:4]),
        (b2.at[0:7], f_ref.at[0:7, 12:16]),
        (mine, f_ref.at[7:15, 4:12]),
        (a1, f_ref.at[7:15, 0:4]),
        (b1, f_ref.at[7:15, 12:16]),
        (following, f_ref.at[15:22, 4:12]),
        (a2.at[7:14], f_ref.at[15:22, 0:4]),
        (b2.at[7:14], f_ref.at[15:22, 12:16]),
    ]
    copies = [pltpu.make_async_copy(x, y, sems.at[i]) for i, (x, y) in enumerate(moves)]
    for copy in copies:
        copy.start()

    for copy in copies[:3]:
        copy.wait()
    lane = lax.broadcasted_iota(jnp.int32, (CH, LANES), 1)
    low = (lane & 7) < 4

    def unpack(g, carry):
        rl = rl_ref[g].astype(jnp.float32)
        rr = rr_ref[g].astype(jnp.float32)
        edge[2 * g] = jnp.where(low, rl, rr)
        edge[2 * g + 1] = jnp.where(low, roll(rl, -4), roll(rr, 4))
        return carry

    lax.fori_loop(0, rl_ref.shape[0], unpack, 0)

    def t_layer(t):
        return t + 2 + 4 * lax.shift_right_logical(t, 2)

    def s_layer(s):
        return s + 4 * lax.shift_right_logical(s + 2, 2)

    def t_halo(t, carry):
        tile = edge[t_layer(t)]
        for q, shift in enumerate((0, 64, -8, 56)):
            t_h[t, q * CH : (q + 1) * CH] = roll(tile, shift).astype(jnp.bfloat16)
        return carry

    lax.fori_loop(0, 12, t_halo, 0)

    def slope_halo(m, row):
        tile = edge[s_layer(m)]
        q = row // 2
        return jnp.concatenate([roll(tile, 64 - 8 * q), roll(tile, -8 * (q + 1))], axis=0)

    def keep_slopes(m, carry):
        slope_h[m] = slope_halo(m + 2, 3)
        return carry

    def field_rows(t, r):
        return f_ref[t_layer(t), pl.ds(r, 4)].reshape(4 * CH, LANES)

    lax.fori_loop(0, 6, keep_slopes, 0)

    def stage_hidden(m, carry):
        def put(p, v):
            slope = f_ref[s_layer(m), pl.ds(2 * p + 1, 2)].reshape(2 * CH, LANES)
            store(hid, m, p, slope.astype(jnp.float32) * v)

        def put_halo(v):
            store_halo(hid_h, m, slope_halo(m, 1) * v)

        convolve_layer(w_ref[0], field_rows, lambda t: t_h[t], m, range(7), put, put_halo)
        return carry

    for start, end, arrived in ((0, 2, 3), (2, 6, 6), (6, 10, 9)):
        for copy in copies[arrived : arrived + 3]:
            copy.wait()
        lax.fori_loop(start, end, stage_hidden, 0)
    early = [
        (hid, hid_out), (hid_h, hid_h_out), (slope_h, slope_h_out),
        (f_ref.at[6:10, 3:13], slope_out.at[0:4]), (f_ref.at[14:16, 3:13], slope_out.at[4:6]),
    ]
    late = [(own_ref, own_out), (own_h, own_h_out)]
    writes = [pltpu.make_async_copy(x, y, out_sems.at[i]) for i, (x, y) in enumerate(early + late)]
    for copy in writes[:5]:
        copy.start()
    sum_acc[...] = jnp.zeros_like(sum_acc)

    def stage_own(m, carry):
        def put(p, v):
            own_ref[m, pl.ds(2 * p - 2, 2)] = v.astype(jnp.bfloat16).reshape(2, CH, LANES)
            square = v * v
            part = square[0:8]
            for q in range(1, 8):
                part = part + square[8 * q : 8 * q + 8]
            sum_acc[...] += part

        def put_halo(v):
            own_h[m] = v

        convolve_layer(
            w_ref[1], rows_of(hid), lambda t: hid_h[t], m + 2, range(1, 5), put, put_halo
        )
        return carry

    lax.fori_loop(0, 4, stage_own, 0)
    for copy in writes[5:]:
        copy.start()
    total = jnp.sum(sum_acc[...], axis=0, keepdims=True)
    for i in range(sum_ref.shape[0]):
        sum_ref[i] = total
    for copy in writes:
        copy.wait()


def first_convs(pieces, rl, rr, weights, spread):
    shape = jax.ShapeDtypeStruct
    anywhere = pl.BlockSpec(memory_space=pl.ANY)
    local = pl.BlockSpec(memory_space=pltpu.VMEM)
    fields = (
        shape((10, 14, CH, LANES), jnp.bfloat16),
        shape((10, 4 * CH, LANES), jnp.bfloat16),
        shape((4, 8, CH, LANES), jnp.bfloat16),
        shape((4, 2 * CH, LANES), jnp.float32),
        shape((6, 10, CH, LANES), jnp.bfloat16),
        shape((6, 2 * CH, LANES), jnp.float32),
    )
    keep = [pltpu.VMEM(fields[i].shape, fields[i].dtype) for i in (0, 1, 2, 3, 5)]
    return pl.pallas_call(
        first_kernel_body,
        out_shape=(*fields, shape((spread, 1, LANES), jnp.float32)),
        in_specs=[anywhere] * 10,
        out_specs=(*([anywhere] * 6), local),
        scratch_shapes=[
            pltpu.VMEM((22, 16, CH, LANES), jnp.bfloat16),
            pltpu.VMEM(rl.shape, rl.dtype),
            pltpu.VMEM(rr.shape, rr.dtype),
            pltpu.VMEM((2, *weights.shape[1:]), weights.dtype),
            pltpu.VMEM((22, CH, LANES), jnp.float32),
            pltpu.VMEM((12, 4 * CH, LANES), jnp.bfloat16),
            *keep,
            pltpu.VMEM((8, LANES), jnp.float32),
            pltpu.SemaphoreType.DMA((12,)),
            pltpu.SemaphoreType.DMA((7,)),
        ],
        compiler_params=pltpu.CompilerParams(vmem_limit_bytes=62 << 20),
        cost_estimate=pl.CostEstimate(flops=8 << 30, bytes_accessed=8 << 20, transcendentals=0),
        name="first_convs",
    )(*pieces, rl, rr, weights)


def second_kernel_body(
    place, hid_in, hid_h_in, own_in, own_h_in, slope_in, slope_h_in, w_in, after, out_ref,
    w_ref, hid, hid_h, own_h, slope_ref, slope_h, img, img_h, pul, pul_h, sems,
):
    moves = [
        (w_in, w_ref), (hid_in, hid), (hid_h_in, hid_h), (own_in, img.at[2:6, 2:10]), (own_h_in, own_h),
        (slope_in, slope_ref), (slope_h_in, slope_h),
    ]
    copies = [pltpu.make_async_copy(x, y, sems.at[i]) for i, (x, y) in enumerate(moves)]
    for copy in copies:
        copy.start()
    for copy in copies[:3]:
        copy.wait()
    wide = lax.broadcasted_iota(jnp.int32, (2 * CH, LANES), 1)
    wide8 = wide & 7
    gx, gy, gz = place[0], place[1], place[2]
    nx, ny, nz = place[3], place[4], place[5]
    top_in = jnp.where(gy > 0, 1.0, 0.0)
    low_in = jnp.where(gy < ny, 1.0, 0.0)
    halo_in = jnp.where(wide8 < 4, jnp.where(gz > 0, 1.0, 0.0), jnp.where(gz < nz, 1.0, 0.0))
    halo_in = jnp.where(wide < 8, halo_in * top_in, halo_in)
    halo_in = jnp.where(wide >= 40, halo_in * low_in, halo_in)

    def image_layer(m, x_in, pairs, merge):
        def put(p, v):
            keep = x_in * (top_in if p == 0 else low_in if p == 5 else 1.0)
            store(img, m, p, v * keep)

        def put_halo(v):
            store_halo(img_h, m, merge(v) * (halo_in * x_in))

        convolve_layer(w_ref[1], rows_of(hid), lambda t: hid_h[t], m, pairs, put, put_halo)

    def stage_ends(i, carry):
        m = jnp.where(i < 2, i, i + 4)
        x_in = jnp.where(((i >= 2) | (gx > 0)) & ((i < 2) | (gx < nx)), 1.0, 0.0)
        image_layer(m, x_in, range(6), lambda v: v)
        return carry

    lax.fori_loop(0, 4, stage_ends, 0)

    for copy in copies[3:]:
        copy.wait()

    def stage_rim(i, carry):
        m = i + 2
        outer = (wide < 8) | (wide >= 40)
        image_layer(m, 1.0, (0, 5), lambda v: jnp.where(outer, v, own_h[i]))
        return carry

    lax.fori_loop(0, 4, stage_rim, 0)

    def stage_pulled(m, carry):
        def put(p, v):
            slope = slope_ref[m, pl.ds(2 * p, 2)].reshape(2 * CH, LANES)
            store(pul, m, p, slope.astype(jnp.float32) * v)

        def put_halo(v):
            store_halo(pul_h, m, slope_h[m] * v)

        convolve_layer(w_ref[2], rows_of(img), lambda t: img_h[t], m, range(5), put, put_halo)
        return carry

    lax.fori_loop(0, 6, stage_pulled, 0)

    def stage_out(m, carry):
        def put(p, v):
            out_ref[m, pl.ds(2 * p, 2)] = v.reshape(2, CH, LANES)

        convolve_layer(w_ref[3], rows_of(pul), lambda t: pul_h[t], m, range(4), put, None)
        return carry

    lax.fori_loop(0, 4, stage_out, 0)


def second_convs(place, fields, weights, after):
    return pl.pallas_call(
        second_kernel_body,
        out_shape=jax.ShapeDtypeStruct((4, 8, CH, LANES), jnp.float32),
        in_specs=[pl.BlockSpec(memory_space=pltpu.SMEM)]
        + [pl.BlockSpec(memory_space=pl.ANY)] * 8,
        scratch_shapes=[
            pltpu.VMEM(weights.shape, weights.dtype),
            *[pltpu.VMEM(f.shape, f.dtype) for i, f in enumerate(fields) if i != 2],
            pltpu.VMEM((8, 12, CH, LANES), jnp.bfloat16),
            pltpu.VMEM((8, 4 * CH, LANES), jnp.bfloat16),
            pltpu.VMEM((6, 10, CH, LANES), jnp.bfloat16),
            pltpu.VMEM((6, 4 * CH, LANES), jnp.bfloat16),
            pltpu.SemaphoreType.DMA((7,)),
        ],
        compiler_params=pltpu.CompilerParams(vmem_limit_bytes=62 << 20),
        cost_estimate=pl.CostEstimate(flops=8 << 30, bytes_accessed=4 << 20, transcendentals=0),
        name="second_convs",
    )(place, *fields, weights, after)


def weights_kernel(k1_ref, k2_ref, w_ref):
    w_ref[...] = jnp.zeros_like(w_ref)
    for which, (ref, adjoint) in enumerate(
        ((k1_ref, False), (k2_ref, False), (k2_ref, True), (k1_ref, True))
    ):
        for tap in range(27):
            a, b, c = tap // 9, tap // 3 % 3, tap % 3
            if adjoint:
                block = ref[26 - tap].astype(jnp.float32).T.astype(jnp.bfloat16)
            else:
                block = ref[tap]
            for row in range(2):
                top = (2 * c + row) * CH
                left = (4 * a + b + row) * CH
                w_ref[which, top : top + CH, left : left + CH] = block


def pair_matrices(first_kernel, second_kernel):
    return pl.pallas_call(
        weights_kernel,
        out_shape=jax.ShapeDtypeStruct((4, 6 * CH, 12 * CH), jnp.bfloat16),
        compiler_params=pltpu.CompilerParams(vmem_limit_bytes=8 << 20),
        cost_estimate=pl.CostEstimate(flops=0, bytes_accessed=4 << 20, transcendentals=0),
        name="pair_matrices",
    )(first_kernel, second_kernel)


def finish_kernel(result, parts, out_ref, norm_ref, block, sems):
    layers = block.shape[0]
    copies = [pltpu.make_async_copy(result.at[x], block.at[x], sems.at[x]) for x in range(layers)]
    for copy in copies:
        copy.start()
    total = jnp.sum(jnp.sum(parts[...], axis=0), axis=1, keepdims=True)
    norm = jnp.sqrt(total + 1e-06)
    norm_ref[0] = norm[0, 0]
    scale = jnp.broadcast_to(norm, (8, LANES))
    for x in range(layers):
        copies[x].wait()
        out_ref[:, x] = block[x].transpose(1, 0, 2) / scale


def finish(result, parts):
    return pl.pallas_call(
        finish_kernel,
        out_shape=(
            jax.ShapeDtypeStruct((CH, 4, 8, LANES), jnp.float32),
            jax.ShapeDtypeStruct((1,), jnp.float32),
        ),
        in_specs=[
            pl.BlockSpec(memory_space=pl.ANY),
            pl.BlockSpec(memory_space=pltpu.VMEM),
        ],
        out_specs=(
            pl.BlockSpec(memory_space=pltpu.VMEM),
            pl.BlockSpec(memory_space=pltpu.SMEM),
        ),
        scratch_shapes=[
            pltpu.VMEM(result.shape, jnp.float32),
            pltpu.SemaphoreType.DMA((result.shape[0],)),
        ],
        compiler_params=pltpu.CompilerParams(vmem_limit_bytes=62 << 20),
        name="finish",
    )(result, parts)


def on_device(tangent, slopes, first_kernel, second_kernel):
    t = tangent.transpose(1, 2, 0, 3)
    s = slopes.transpose(1, 2, 0, 3)
    mine = jnp.concatenate([s[0:3], t, s[3:4]], axis=0)
    prev, following = shift_pair(mine[1:8], mine[0:7], "gx")
    a1, b1 = shift_pair(mine[:, 4:8], mine[:, 0:4], "gy")
    weights = pair_matrices(first_kernel, second_kernel)
    prev, following, a1, b1, weights = lax.optimization_barrier(
        (prev, following, a1, b1, weights)
    )
    low, top = edge_rows(prev, following)
    a2, b2 = shift_pair(low, top, "gy")
    left_edge, right_edge = pack_edges(a2, b2, pack_mid(prev, mine, following, a1, b1))
    rl, rr = shift_pair(right_edge, left_edge, "gz")
    plane = lax.axis_size(("gy", "gz"))
    pieces = (prev, mine, following, a1, b1, a2, b2)
    *fields, spread = first_convs(pieces, rl, rr, weights, plane)

    place = jnp.stack(
        [lax.axis_index(a) for a in ALL] + [jnp.int32(lax.axis_size(a) - 1) for a in ALL]
    ).astype(jnp.int32)
    parts = lax.all_to_all(spread, ("gy", "gz"), 0, 0, tiled=True)
    part = jnp.sum(parts, axis=0, keepdims=True)
    result = second_convs(place, fields, weights, part)
    count = lax.axis_size("gx")
    parts = lax.all_to_all(jnp.broadcast_to(part, (count, 1, LANES)), "gx", 0, 0, tiled=True)
    return finish(result, parts)


def solution(mesh):
    return jax.shard_map(
        on_device,
        mesh=mesh,
        in_specs=(P(None, "gx", "gy", "gz"), P(None, "gx", "gy", "gz"), P(), P()),
        out_specs=(P(None, "gx", "gy", "gz"), P()),
        check_vma=False,
    )
```

```python
import jax
import jax.numpy as jnp
from jax import lax
from jax.experimental import pallas as pl
from jax.experimental.pallas import tpu as pltpu
from jax.sharding import PartitionSpec as P

ALL = ("gx", "gy", "gz")
CH = 32
LANES = 128


def shift_pair(up, down, axis):
    ends = lax.axis_size(axis) - 1
    from_prev = lax.ppermute(up, axis, [(i, i + 1) for i in range(ends)])
    from_next = lax.ppermute(down, axis, [(i + 1, i) for i in range(ends)])
    return from_prev, from_next


def roll(v, shift):
    return pltpu.roll(v, shift % LANES, 1)


def slot_of(row):
    return 8 * (row % 2) + row // 2


def gather_edges(tile, rows, load, lane):
    for row in rows:
        slot = slot_of(row)
        rolled = roll(load(row).astype(jnp.float32), 8 * slot + 4)
        tile = jnp.where(lane // 8 == slot, rolled, tile)
    return tile


def rows_kernel(prev_ref, next_ref, low_ref, top_ref):
    low_ref[0:7] = prev_ref[:, 4:8]
    low_ref[7:14] = next_ref[:, 4:8]
    top_ref[0:7] = prev_ref[:, 0:4]
    top_ref[7:14] = next_ref[:, 0:4]


def edge_rows(prev, following):
    out = jax.ShapeDtypeStruct((14, 4, CH, LANES), jnp.bfloat16)
    return pl.pallas_call(
        rows_kernel,
        out_shape=(out, out),
        compiler_params=pltpu.CompilerParams(vmem_limit_bytes=16 << 20),
        cost_estimate=pl.CostEstimate(flops=0, bytes_accessed=1 << 21, transcendentals=0),
        name="edge_rows",
    )(prev, following)


OUTER = list(range(4)) + list(range(12, 16))


def pack_mid_kernel(prev_ref, mine_ref, next_ref, a1, b1, tile_ref):
    lane = lax.broadcasted_iota(jnp.int32, (CH, LANES), 1)
    none = jnp.zeros((CH, LANES), jnp.float32)

    def layers(ref, base):
        def body(i, carry):
            tile_ref[base + i] = gather_edges(none, range(4, 12), lambda r: ref[i, r - 4], lane)
            return carry

        lax.fori_loop(0, ref.shape[0], body, 0)

    def own(i, carry):
        def load(r):
            if 4 <= r < 12:
                return mine_ref[i, r - 4]
            return a1[i, r] if r < 4 else b1[i, r - 12]

        tile_ref[7 + i] = gather_edges(none, range(16), load, lane)
        return carry

    layers(prev_ref, 0)
    lax.fori_loop(0, 8, own, 0)
    layers(next_ref, 15)


def pack_mid(prev, mine, following, a1, b1):
    return pl.pallas_call(
        pack_mid_kernel,
        out_shape=jax.ShapeDtypeStruct((22, CH, LANES), jnp.float32),
        compiler_params=pltpu.CompilerParams(vmem_limit_bytes=16 << 20),
        cost_estimate=pl.CostEstimate(flops=0, bytes_accessed=1 << 21, transcendentals=0),
        name="pack_mid",
    )(prev, mine, following, a1, b1)


def pack_kernel(a2, b2, tile_ref, left_ref, right_ref, full):
    lane = lax.broadcasted_iota(jnp.int32, (CH, LANES), 1)
    low = (lane & 7) < 4
    full[7:15] = tile_ref[7:15]

    def received(i, carry):
        at = jnp.where(i < 7, i, i + 8)
        load = lambda r: a2[i, r] if r < 4 else b2[i, r - 12]
        full[at] = gather_edges(tile_ref[at], OUTER, load, lane)
        return carry

    lax.fori_loop(0, 14, received, 0, unroll=True)

    def group(g, carry):
        one, two = full[2 * g], full[2 * g + 1]
        right_ref[g] = jnp.where(low, one, roll(two, 4)).astype(jnp.bfloat16)
        left_ref[g] = jnp.where(low, roll(two, -4), one).astype(jnp.bfloat16)
        return carry

    lax.fori_loop(0, left_ref.shape[0], group, 0, unroll=True)


def pack_edges(a2, b2, tiles):
    out = jax.ShapeDtypeStruct((11, CH, LANES), jnp.bfloat16)
    return pl.pallas_call(
        pack_kernel,
        out_shape=(out, out),
        scratch_shapes=[pltpu.VMEM((22, CH, LANES), jnp.float32)],
        compiler_params=pltpu.CompilerParams(vmem_limit_bytes=16 << 20),
        cost_estimate=pl.CostEstimate(flops=0, bytes_accessed=1 << 21, transcendentals=0),
        name="pack_edges",
    )(a2, b2, tiles)


def convolve_layer(w, get, get_halo, m, pairs, put, put_halo):
    wide = lax.broadcasted_iota(jnp.int32, (2 * CH, LANES), 1)
    wide8 = wide & 7
    first = wide == 0
    n = 2 * CH

    def columns(p):
        if p < 0:
            return jnp.concatenate([get_halo(m + a) for a in range(3)], axis=0)
        return jnp.concatenate([get(m + a, 2 * p) for a in range(3)], axis=0)

    cross = None
    halo = None
    tiles = [-1] + list(pairs)
    for start in range(0, len(tiles), 2):
        here = tiles[start : start + 2]
        rhs = jnp.concatenate([columns(p) for p in here], axis=1)
        g = jnp.dot(w, rhs, preferred_element_type=jnp.float32)
        for k, p in enumerate(here):
            part = g[:, k * LANES : (k + 1) * LANES]
            before = roll(part[:n], 1)
            after = roll(part[2 * n :], -1)
            if p < 0:
                cross = jnp.where(wide8 == 4, before, after)
                halo = (
                    part[n : 2 * n]
                    + jnp.where(wide8 == 4, 0.0, before)
                    + jnp.where(wide8 == 3, 0.0, after)
                )
                continue
            mine = roll(cross, -(8 * p + 4))
            own = (
                part[n : 2 * n]
                + jnp.where(first, mine, before)
                + jnp.where(wide == LANES - 1, mine, after)
            )
            put(p, own)
            if put_halo is not None:
                give = roll(jnp.where(first, before, after), 8 * p + 4)
                halo = halo + jnp.where((wide == 8 * p + 3) | (wide == 8 * p + 4), give, 0.0)
    if put_halo is not None:
        put_halo(halo)


def store_halo(ref, m, v):
    for q, piece in enumerate((v[:CH], v[CH:], roll(v[:CH], -8), roll(v[CH:], -8))):
        ref[m, q * CH : (q + 1) * CH] = piece.astype(jnp.bfloat16)


def store(ref, m, p, v):
    ref[m, pl.ds(2 * p, 2)] = v.astype(jnp.bfloat16).reshape(2, CH, LANES)


def rows_of(ref):
    return lambda t, r: ref[t, pl.ds(r, 4)].reshape(4 * CH, LANES)


def first_kernel_body(
    prev, mine, following, a1, b1, a2, b2, rl_in, rr_in, w_in,
    hid_out, hid_h_out, own_out, own_h_out, slope_out, slope_h_out, sum_ref,
    f_ref, rl_ref, rr_ref, w_ref, edge, t_h, hid, hid_h, own_ref, own_h, slope_h, sum_acc, sems, out_sems,
):
    moves = [
        (rl_in, rl_ref),
        (rr_in, rr_ref),
        (w_in.at[0:2], w_ref),
        (prev, f_ref.at[0:7, 4:12]),
        (a2.at[0:7], f_ref.at[0:7, 0:4]),
        (b2.at[0:7], f_ref.at[0:7, 12:16]),
        (mine, f_ref.at[7:15, 4:12]),
        (a1, f_ref.at[7:15, 0:4]),
        (b1, f_ref.at[7:15, 12:16]),
        (following, f_ref.at[15:22, 4:12]),
        (a2.at[7:14], f_ref.at[15:22, 0:4]),
        (b2.at[7:14], f_ref.at[15:22, 12:16]),
    ]
    copies = [pltpu.make_async_copy(x, y, sems.at[i]) for i, (x, y) in enumerate(moves)]
    for copy in copies:
        copy.start()

    for copy in copies[:3]:
        copy.wait()
    lane = lax.broadcasted_iota(jnp.int32, (CH, LANES), 1)
    low = (lane & 7) < 4

    def unpack(g, carry):
        rl = rl_ref[g].astype(jnp.float32)
        rr = rr_ref[g].astype(jnp.float32)
        edge[2 * g] = jnp.where(low, rl, rr)
        edge[2 * g + 1] = jnp.where(low, roll(rl, -4), roll(rr, 4))
        return carry

    lax.fori_loop(0, rl_ref.shape[0], unpack, 0, unroll=True)

    def t_layer(t):
        return t + 2 + 4 * lax.shift_right_logical(t, 2)

    def s_layer(s):
        return s + 4 * lax.shift_right_logical(s + 2, 2)

    def t_halo(t, carry):
        tile = edge[t_layer(t)]
        for q, shift in enumerate((0, 64, -8, 56)):
            t_h[t, q * CH : (q + 1) * CH] = roll(tile, shift).astype(jnp.bfloat16)
        return carry

    lax.fori_loop(0, 12, t_halo, 0, unroll=True)

    def slope_halo(m, row):
        tile = edge[s_layer(m)]
        q = row // 2
        return jnp.concatenate([roll(tile, 64 - 8 * q), roll(tile, -8 * (q + 1))], axis=0)

    def keep_slopes(m, carry):
        slope_h[m] = slope_halo(m + 2, 3)
        return carry

    def field_rows(t, r):
        return f_ref[t_layer(t), pl.ds(r, 4)].reshape(4 * CH, LANES)

    lax.fori_loop(0, 6, keep_slopes, 0, unroll=True)

    def stage_hidden(m, carry):
        def put(p, v):
            slope = f_ref[s_layer(m), pl.ds(2 * p + 1, 2)].reshape(2 * CH, LANES)
            store(hid, m, p, slope.astype(jnp.float32) * v)

        def put_halo(v):
            store_halo(hid_h, m, slope_halo(m, 1) * v)

        convolve_layer(w_ref[0], field_rows, lambda t: t_h[t], m, range(7), put, put_halo)
        return carry

    for start, end, arrived in ((0, 2, 3), (2, 6, 6), (6, 10, 9)):
        for copy in copies[arrived : arrived + 3]:
            copy.wait()
        lax.fori_loop(start, end, stage_hidden, 0, unroll=True)
    early = [
        (hid, hid_out), (hid_h, hid_h_out), (slope_h, slope_h_out),
        (f_ref.at[6:10, 3:13], slope_out.at[0:4]), (f_ref.at[14:16, 3:13], slope_out.at[4:6]),
    ]
    late = [(own_ref, own_out), (own_h, own_h_out)]
    writes = [pltpu.make_async_copy(x, y, out_sems.at[i]) for i, (x, y) in enumerate(early + late)]
    for copy in writes[:5]:
        copy.start()
    sum_acc[...] = jnp.zeros_like(sum_acc)

    def stage_own(m, carry):
        def put(p, v):
            own_ref[m, pl.ds(2 * p - 2, 2)] = v.astype(jnp.bfloat16).reshape(2, CH, LANES)
            square = v * v
            part = square[0:8]
            for q in range(1, 8):
                part = part + square[8 * q : 8 * q + 8]
            sum_acc[...] += part

        def put_halo(v):
            own_h[m] = v

        convolve_layer(
            w_ref[1], rows_of(hid), lambda t: hid_h[t], m + 2, range(1, 5), put, put_halo
        )
        return carry

    lax.fori_loop(0, 4, stage_own, 0, unroll=True)
    for copy in writes[5:]:
        copy.start()
    total = jnp.sum(sum_acc[...], axis=0, keepdims=True)
    for i in range(sum_ref.shape[0]):
        sum_ref[i] = total
    for copy in writes:
        copy.wait()


def first_convs(pieces, rl, rr, weights, spread):
    shape = jax.ShapeDtypeStruct
    anywhere = pl.BlockSpec(memory_space=pl.ANY)
    local = pl.BlockSpec(memory_space=pltpu.VMEM)
    fields = (
        shape((10, 14, CH, LANES), jnp.bfloat16),
        shape((10, 4 * CH, LANES), jnp.bfloat16),
        shape((4, 8, CH, LANES), jnp.bfloat16),
        shape((4, 2 * CH, LANES), jnp.float32),
        shape((6, 10, CH, LANES), jnp.bfloat16),
        shape((6, 2 * CH, LANES), jnp.float32),
    )
    keep = [pltpu.VMEM(fields[i].shape, fields[i].dtype) for i in (0, 1, 2, 3, 5)]
    return pl.pallas_call(
        first_kernel_body,
        out_shape=(*fields, shape((spread, 1, LANES), jnp.float32)),
        in_specs=[anywhere] * 10,
        out_specs=(*([anywhere] * 6), local),
        scratch_shapes=[
            pltpu.VMEM((22, 16, CH, LANES), jnp.bfloat16),
            pltpu.VMEM(rl.shape, rl.dtype),
            pltpu.VMEM(rr.shape, rr.dtype),
            pltpu.VMEM((2, *weights.shape[1:]), weights.dtype),
            pltpu.VMEM((22, CH, LANES), jnp.float32),
            pltpu.VMEM((12, 4 * CH, LANES), jnp.bfloat16),
            *keep,
            pltpu.VMEM((8, LANES), jnp.float32),
            pltpu.SemaphoreType.DMA((12,)),
            pltpu.SemaphoreType.DMA((7,)),
        ],
        compiler_params=pltpu.CompilerParams(vmem_limit_bytes=62 << 20),
        cost_estimate=pl.CostEstimate(flops=8 << 30, bytes_accessed=8 << 20, transcendentals=0),
        name="first_convs",
    )(*pieces, rl, rr, weights)


def second_kernel_body(
    place, hid_in, hid_h_in, own_in, own_h_in, slope_in, slope_h_in, w_in, after, out_ref,
    w_ref, hid, hid_h, own_h, slope_ref, slope_h, img, img_h, pul, pul_h, sems,
):
    moves = [
        (w_in, w_ref), (hid_in, hid), (hid_h_in, hid_h), (own_in, img.at[2:6, 2:10]), (own_h_in, own_h),
        (slope_in, slope_ref), (slope_h_in, slope_h),
    ]
    copies = [pltpu.make_async_copy(x, y, sems.at[i]) for i, (x, y) in enumerate(moves)]
    for copy in copies:
        copy.start()
    for copy in copies[:3]:
        copy.wait()
    wide = lax.broadcasted_iota(jnp.int32, (2 * CH, LANES), 1)
    wide8 = wide & 7
    gx, gy, gz = place[0], place[1], place[2]
    nx, ny, nz = place[3], place[4], place[5]
    top_in = jnp.where(gy > 0, 1.0, 0.0)
    low_in = jnp.where(gy < ny, 1.0, 0.0)
    halo_in = jnp.where(wide8 < 4, jnp.where(gz > 0, 1.0, 0.0), jnp.where(gz < nz, 1.0, 0.0))
    halo_in = jnp.where(wide < 8, halo_in * top_in, halo_in)
    halo_in = jnp.where(wide >= 40, halo_in * low_in, halo_in)

    def image_layer(m, x_in, pairs, merge):
        def put(p, v):
            keep = x_in * (top_in if p == 0 else low_in if p == 5 else 1.0)
            store(img, m, p, v * keep)

        def put_halo(v):
            store_halo(img_h, m, merge(v) * (halo_in * x_in))

        convolve_layer(w_ref[1], rows_of(hid), lambda t: hid_h[t], m, pairs, put, put_halo)

    def stage_ends(i, carry):
        m = jnp.where(i < 2, i, i + 4)
        x_in = jnp.where(((i >= 2) | (gx > 0)) & ((i < 2) | (gx < nx)), 1.0, 0.0)
        image_layer(m, x_in, range(6), lambda v: v)
        return carry

    lax.fori_loop(0, 4, stage_ends, 0, unroll=True)

    for copy in copies[3:]:
        copy.wait()

    def stage_rim(i, carry):
        m = i + 2
        outer = (wide < 8) | (wide >= 40)
        image_layer(m, 1.0, (0, 5), lambda v: jnp.where(outer, v, own_h[i]))
        return carry

    lax.fori_loop(0, 4, stage_rim, 0, unroll=True)

    def stage_pulled(m, carry):
        def put(p, v):
            slope = slope_ref[m, pl.ds(2 * p, 2)].reshape(2 * CH, LANES)
            store(pul, m, p, slope.astype(jnp.float32) * v)

        def put_halo(v):
            store_halo(pul_h, m, slope_h[m] * v)

        convolve_layer(w_ref[2], rows_of(img), lambda t: img_h[t], m, range(5), put, put_halo)
        return carry

    lax.fori_loop(0, 6, stage_pulled, 0, unroll=True)

    def stage_out(m, carry):
        def put(p, v):
            out_ref[m, pl.ds(2 * p, 2)] = v.reshape(2, CH, LANES)

        convolve_layer(w_ref[3], rows_of(pul), lambda t: pul_h[t], m, range(4), put, None)
        return carry

    lax.fori_loop(0, 4, stage_out, 0, unroll=True)


def second_convs(place, fields, weights, after):
    return pl.pallas_call(
        second_kernel_body,
        out_shape=jax.ShapeDtypeStruct((4, 8, CH, LANES), jnp.float32),
        in_specs=[pl.BlockSpec(memory_space=pltpu.SMEM)]
        + [pl.BlockSpec(memory_space=pl.ANY)] * 8,
        scratch_shapes=[
            pltpu.VMEM(weights.shape, weights.dtype),
            *[pltpu.VMEM(f.shape, f.dtype) for i, f in enumerate(fields) if i != 2],
            pltpu.VMEM((8, 12, CH, LANES), jnp.bfloat16),
            pltpu.VMEM((8, 4 * CH, LANES), jnp.bfloat16),
            pltpu.VMEM((6, 10, CH, LANES), jnp.bfloat16),
            pltpu.VMEM((6, 4 * CH, LANES), jnp.bfloat16),
            pltpu.SemaphoreType.DMA((7,)),
        ],
        compiler_params=pltpu.CompilerParams(vmem_limit_bytes=62 << 20),
        cost_estimate=pl.CostEstimate(flops=8 << 30, bytes_accessed=4 << 20, transcendentals=0),
        name="second_convs",
    )(place, *fields, weights, after)


def weights_kernel(k1_ref, k2_ref, w_ref):
    w_ref[...] = jnp.zeros_like(w_ref)
    for which, (ref, adjoint) in enumerate(
        ((k1_ref, False), (k2_ref, False), (k2_ref, True), (k1_ref, True))
    ):
        for tap in range(27):
            a, b, c = tap // 9, tap // 3 % 3, tap % 3
            if adjoint:
                block = ref[26 - tap].astype(jnp.float32).T.astype(jnp.bfloat16)
            else:
                block = ref[tap]
            for row in range(2):
                top = (2 * c + row) * CH
                left = (4 * a + b + row) * CH
                w_ref[which, top : top + CH, left : left + CH] = block


def pair_matrices(first_kernel, second_kernel):
    return pl.pallas_call(
        weights_kernel,
        out_shape=jax.ShapeDtypeStruct((4, 6 * CH, 12 * CH), jnp.bfloat16),
        compiler_params=pltpu.CompilerParams(vmem_limit_bytes=8 << 20),
        cost_estimate=pl.CostEstimate(flops=0, bytes_accessed=4 << 20, transcendentals=0),
        name="pair_matrices",
    )(first_kernel, second_kernel)


def finish_kernel(result, parts, out_ref, norm_ref):
    total = jnp.sum(jnp.sum(parts[...], axis=0), axis=1, keepdims=True)
    norm = jnp.sqrt(total + 1e-06)
    norm_ref[0] = norm[0, 0]
    scale = jnp.broadcast_to(norm, (8, LANES))
    for x in range(result.shape[0]):
        out_ref[:, x] = result[x].transpose(1, 0, 2) / scale


def finish(result, parts):
    return pl.pallas_call(
        finish_kernel,
        out_shape=(
            jax.ShapeDtypeStruct((CH, 4, 8, LANES), jnp.float32),
            jax.ShapeDtypeStruct((1,), jnp.float32),
        ),
        out_specs=(
            pl.BlockSpec(memory_space=pltpu.VMEM),
            pl.BlockSpec(memory_space=pltpu.SMEM),
        ),
        compiler_params=pltpu.CompilerParams(vmem_limit_bytes=16 << 20),
        name="finish",
    )(result, parts)


def on_device(tangent, slopes, first_kernel, second_kernel):
    t = tangent.transpose(1, 2, 0, 3)
    s = slopes.transpose(1, 2, 0, 3)
    mine = jnp.concatenate([s[0:3], t, s[3:4]], axis=0)
    prev, following = shift_pair(mine[1:8], mine[0:7], "gx")
    a1, b1 = shift_pair(mine[:, 4:8], mine[:, 0:4], "gy")
    weights = pair_matrices(first_kernel, second_kernel)
    prev, following, a1, b1, weights = lax.optimization_barrier(
        (prev, following, a1, b1, weights)
    )
    low, top = edge_rows(prev, following)
    a2, b2 = shift_pair(low, top, "gy")
    left_edge, right_edge = pack_edges(a2, b2, pack_mid(prev, mine, following, a1, b1))
    rl, rr = shift_pair(right_edge, left_edge, "gz")
    plane = lax.axis_size(("gy", "gz"))
    pieces = (prev, mine, following, a1, b1, a2, b2)
    *fields, spread = first_convs(pieces, rl, rr, weights, plane)

    place = jnp.stack(
        [lax.axis_index(a) for a in ALL] + [jnp.int32(lax.axis_size(a) - 1) for a in ALL]
    ).astype(jnp.int32)
    parts = lax.all_to_all(spread, ("gy", "gz"), 0, 0, tiled=True)
    part = jnp.sum(parts, axis=0, keepdims=True)
    result = second_convs(place, fields, weights, part)
    count = lax.axis_size("gx")
    parts = lax.all_to_all(jnp.broadcast_to(part, (count, 1, LANES)), "gx", 0, 0, tiled=True)
    return finish(result, parts)


def solution(mesh):
    return jax.shard_map(
        on_device,
        mesh=mesh,
        in_specs=(P(None, "gx", "gy", "gz"), P(None, "gx", "gy", "gz"), P(), P()),
        out_specs=(P(None, "gx", "gy", "gz"), P()),
        check_vma=False,
    )
```

```python
import jax
import jax.numpy as jnp
from jax import lax
from jax.experimental import pallas as pl
from jax.experimental.pallas import tpu as pltpu
from jax.sharding import PartitionSpec as P

ALL = ("gx", "gy", "gz")
CH = 32
LANES = 128


def shift_pair(up, down, axis):
    ends = lax.axis_size(axis) - 1
    from_prev = lax.ppermute(up, axis, [(i, i + 1) for i in range(ends)])
    from_next = lax.ppermute(down, axis, [(i + 1, i) for i in range(ends)])
    return from_prev, from_next


def roll(v, shift):
    return pltpu.roll(v, shift % LANES, 1)


def slot_of(row):
    return 8 * (row % 2) + row // 2


def gather_edges(tile, rows, load, lane):
    for row in rows:
        slot = slot_of(row)
        rolled = roll(load(row).astype(jnp.float32), 8 * slot + 4)
        tile = jnp.where(lane // 8 == slot, rolled, tile)
    return tile


def rows_kernel(prev_ref, next_ref, low_ref, top_ref):
    low_ref[0:7] = prev_ref[:, 4:8]
    low_ref[7:14] = next_ref[:, 4:8]
    top_ref[0:7] = prev_ref[:, 0:4]
    top_ref[7:14] = next_ref[:, 0:4]


def edge_rows(prev, following):
    out = jax.ShapeDtypeStruct((14, 4, CH, LANES), jnp.bfloat16)
    return pl.pallas_call(
        rows_kernel,
        out_shape=(out, out),
        compiler_params=pltpu.CompilerParams(vmem_limit_bytes=16 << 20),
        cost_estimate=pl.CostEstimate(flops=0, bytes_accessed=1 << 21, transcendentals=0),
        name="edge_rows",
    )(prev, following)


OUTER = list(range(4)) + list(range(12, 16))


def pack_mid_kernel(prev_ref, mine_ref, next_ref, a1, b1, tile_ref):
    lane = lax.broadcasted_iota(jnp.int32, (CH, LANES), 1)
    none = jnp.zeros((CH, LANES), jnp.float32)

    def layers(ref, base):
        def body(i, carry):
            tile_ref[base + i] = gather_edges(none, range(4, 12), lambda r: ref[i, r - 4], lane)
            return carry

        lax.fori_loop(0, ref.shape[0], body, 0)

    def own(i, carry):
        def load(r):
            if 4 <= r < 12:
                return mine_ref[i, r - 4]
            return a1[i, r] if r < 4 else b1[i, r - 12]

        tile_ref[7 + i] = gather_edges(none, range(16), load, lane)
        return carry

    layers(prev_ref, 0)
    lax.fori_loop(0, 8, own, 0)
    layers(next_ref, 15)


def pack_mid(prev, mine, following, a1, b1):
    return pl.pallas_call(
        pack_mid_kernel,
        out_shape=jax.ShapeDtypeStruct((22, CH, LANES), jnp.float32),
        compiler_params=pltpu.CompilerParams(vmem_limit_bytes=16 << 20),
        cost_estimate=pl.CostEstimate(flops=0, bytes_accessed=1 << 21, transcendentals=0),
        name="pack_mid",
    )(prev, mine, following, a1, b1)


def pack_kernel(a2, b2, tile_ref, left_ref, right_ref, full):
    lane = lax.broadcasted_iota(jnp.int32, (CH, LANES), 1)
    low = (lane & 7) < 4
    full[7:15] = tile_ref[7:15]

    def received(i, carry):
        at = jnp.where(i < 7, i, i + 8)
        load = lambda r: a2[i, r] if r < 4 else b2[i, r - 12]
        full[at] = gather_edges(tile_ref[at], OUTER, load, lane)
        return carry

    lax.fori_loop(0, 14, received, 0, unroll=True)

    def group(g, carry):
        one, two = full[2 * g], full[2 * g + 1]
        right_ref[g] = jnp.where(low, one, roll(two, 4)).astype(jnp.bfloat16)
        left_ref[g] = jnp.where(low, roll(two, -4), one).astype(jnp.bfloat16)
        return carry

    lax.fori_loop(0, left_ref.shape[0], group, 0, unroll=True)


def pack_edges(a2, b2, tiles):
    out = jax.ShapeDtypeStruct((11, CH, LANES), jnp.bfloat16)
    return pl.pallas_call(
        pack_kernel,
        out_shape=(out, out),
        scratch_shapes=[pltpu.VMEM((22, CH, LANES), jnp.float32)],
        compiler_params=pltpu.CompilerParams(vmem_limit_bytes=16 << 20),
        cost_estimate=pl.CostEstimate(flops=0, bytes_accessed=1 << 21, transcendentals=0),
        name="pack_edges",
    )(a2, b2, tiles)


def convolve_layer(w, get, get_halo, m, pairs, put, put_halo):
    wide = lax.broadcasted_iota(jnp.int32, (2 * CH, LANES), 1)
    wide8 = wide & 7
    first = wide == 0
    n = 2 * CH

    def columns(p):
        if p < 0:
            return jnp.concatenate([get_halo(m + a) for a in range(3)], axis=0)
        return jnp.concatenate([get(m + a, 2 * p) for a in range(3)], axis=0)

    cross = None
    halo = None
    tiles = [-1] + list(pairs)
    for start in range(0, len(tiles), 2):
        here = tiles[start : start + 2]
        rhs = jnp.concatenate([columns(p) for p in here], axis=1)
        g = jnp.dot(w, rhs, preferred_element_type=jnp.float32)
        for k, p in enumerate(here):
            part = g[:, k * LANES : (k + 1) * LANES]
            before = roll(part[:n], 1)
            after = roll(part[2 * n :], -1)
            if p < 0:
                cross = jnp.where(wide8 == 4, before, after)
                halo = (
                    part[n : 2 * n]
                    + jnp.where(wide8 == 4, 0.0, before)
                    + jnp.where(wide8 == 3, 0.0, after)
                )
                continue
            mine = roll(cross, -(8 * p + 4))
            own = (
                part[n : 2 * n]
                + jnp.where(first, mine, before)
                + jnp.where(wide == LANES - 1, mine, after)
            )
            put(p, own)
            if put_halo is not None:
                give = roll(jnp.where(first, before, after), 8 * p + 4)
                halo = halo + jnp.where((wide == 8 * p + 3) | (wide == 8 * p + 4), give, 0.0)
    if put_halo is not None:
        put_halo(halo)


def store_halo(ref, m, v):
    for q, piece in enumerate((v[:CH], v[CH:], roll(v[:CH], -8), roll(v[CH:], -8))):
        ref[m, q * CH : (q + 1) * CH] = piece.astype(jnp.bfloat16)


def store(ref, m, p, v):
    ref[m, pl.ds(2 * p, 2)] = v.astype(jnp.bfloat16).reshape(2, CH, LANES)


def rows_of(ref):
    return lambda t, r: ref[t, pl.ds(r, 4)].reshape(4 * CH, LANES)


OUTER_LAYERS = (0, 1, 8, 9)


def first_kernel_body(
    prev, mine, following, a1, b1, a2, b2, rl_in, rr_in, w_in,
    hid_out, hid_h_out, own_out, own_h_out, slope_out, slope_h_out, t_h_out, far_h_out, sum_ref,
    f_ref, rl_ref, rr_ref, w_ref, edge, t_h, hid, hid_h, own_ref, own_h, slope_h, far_h, sum_acc, sems, out_sems,
):
    moves = [
        (rl_in, rl_ref),
        (rr_in, rr_ref),
        (w_in.at[0:2], w_ref),
        (prev, f_ref.at[0:7, 4:12]),
        (a2.at[0:7], f_ref.at[0:7, 0:4]),
        (b2.at[0:7], f_ref.at[0:7, 12:16]),
        (mine, f_ref.at[7:15, 4:12]),
        (a1, f_ref.at[7:15, 0:4]),
        (b1, f_ref.at[7:15, 12:16]),
        (following, f_ref.at[15:22, 4:12]),
        (a2.at[7:14], f_ref.at[15:22, 0:4]),
        (b2.at[7:14], f_ref.at[15:22, 12:16]),
    ]
    copies = [pltpu.make_async_copy(x, y, sems.at[i]) for i, (x, y) in enumerate(moves)]
    for copy in copies:
        copy.start()

    for copy in copies[:3]:
        copy.wait()
    lane = lax.broadcasted_iota(jnp.int32, (CH, LANES), 1)
    low = (lane & 7) < 4

    def unpack(g, carry):
        rl = rl_ref[g].astype(jnp.float32)
        rr = rr_ref[g].astype(jnp.float32)
        edge[2 * g] = jnp.where(low, rl, rr)
        edge[2 * g + 1] = jnp.where(low, roll(rl, -4), roll(rr, 4))
        return carry

    lax.fori_loop(0, rl_ref.shape[0], unpack, 0, unroll=True)

    def t_layer(t):
        return t + 2 + 4 * lax.shift_right_logical(t, 2)

    def s_layer(s):
        return s + 4 * lax.shift_right_logical(s + 2, 2)

    def t_halo(t, carry):
        tile = edge[t_layer(t)]
        for q, shift in enumerate((0, 64, -8, 56)):
            t_h[t, q * CH : (q + 1) * CH] = roll(tile, shift).astype(jnp.bfloat16)
        return carry

    lax.fori_loop(0, 12, t_halo, 0, unroll=True)

    def slope_halo(m, row):
        tile = edge[s_layer(m)]
        q = row // 2
        return jnp.concatenate([roll(tile, 64 - 8 * q), roll(tile, -8 * (q + 1))], axis=0)

    def keep_slopes(m, carry):
        slope_h[m] = slope_halo(m + 2, 3)
        return carry

    def field_rows(t, r):
        return f_ref[t_layer(t), pl.ds(r, 4)].reshape(4 * CH, LANES)

    lax.fori_loop(0, 6, keep_slopes, 0, unroll=True)
    for i, m in enumerate(OUTER_LAYERS):
        far_h[i] = slope_halo(m, 1)

    def stage_hidden(m, carry):
        def put(p, v):
            slope = f_ref[s_layer(m), pl.ds(2 * p + 1, 2)].reshape(2 * CH, LANES)
            store(hid, m, p, slope.astype(jnp.float32) * v)

        def put_halo(v):
            store_halo(hid_h, m, slope_halo(m, 1) * v)

        convolve_layer(w_ref[0], field_rows, lambda t: t_h[t], m, range(7), put, put_halo)
        return carry

    for start, end, first, last in ((2, 6, 3, 9), (6, 8, 9, 12)):
        for copy in copies[first:last]:
            copy.wait()
        lax.fori_loop(start, end, stage_hidden, 0, unroll=True)
    early = [
        (hid.at[2:8], hid_out.at[2:8]), (hid_h.at[2:8], hid_h_out.at[2:8]),
        (slope_h, slope_h_out), (t_h, t_h_out), (far_h, far_h_out),
        (f_ref.at[6:10, 3:13], slope_out.at[0:4]), (f_ref.at[14:16, 3:13], slope_out.at[4:6]),
    ]
    late = [(own_ref, own_out), (own_h, own_h_out)]
    writes = [pltpu.make_async_copy(x, y, out_sems.at[i]) for i, (x, y) in enumerate(early + late)]
    for copy in writes[:7]:
        copy.start()
    sum_acc[...] = jnp.zeros_like(sum_acc)

    def stage_own(m, carry):
        def put(p, v):
            own_ref[m, pl.ds(2 * p - 2, 2)] = v.astype(jnp.bfloat16).reshape(2, CH, LANES)
            square = v * v
            part = square[0:8]
            for q in range(1, 8):
                part = part + square[8 * q : 8 * q + 8]
            sum_acc[...] += part

        def put_halo(v):
            own_h[m] = v

        convolve_layer(
            w_ref[1], rows_of(hid), lambda t: hid_h[t], m + 2, range(1, 5), put, put_halo
        )
        return carry

    lax.fori_loop(0, 4, stage_own, 0, unroll=True)
    for copy in writes[7:]:
        copy.start()
    total = jnp.sum(sum_acc[...], axis=0, keepdims=True)
    for i in range(sum_ref.shape[0]):
        sum_ref[i] = total
    for copy in writes:
        copy.wait()


def first_convs(pieces, rl, rr, weights, spread):
    shape = jax.ShapeDtypeStruct
    anywhere = pl.BlockSpec(memory_space=pl.ANY)
    local = pl.BlockSpec(memory_space=pltpu.VMEM)
    fields = (
        shape((10, 14, CH, LANES), jnp.bfloat16),
        shape((10, 4 * CH, LANES), jnp.bfloat16),
        shape((4, 8, CH, LANES), jnp.bfloat16),
        shape((4, 2 * CH, LANES), jnp.float32),
        shape((6, 10, CH, LANES), jnp.bfloat16),
        shape((6, 2 * CH, LANES), jnp.float32),
        shape((12, 4 * CH, LANES), jnp.bfloat16),
        shape((4, 2 * CH, LANES), jnp.float32),
    )
    keep = [pltpu.VMEM(fields[i].shape, fields[i].dtype) for i in (0, 1, 2, 3, 5, 7)]
    return pl.pallas_call(
        first_kernel_body,
        out_shape=(*fields, shape((spread, 1, LANES), jnp.float32)),
        in_specs=[anywhere] * 10,
        out_specs=(*([anywhere] * 8), local),
        scratch_shapes=[
            pltpu.VMEM((22, 16, CH, LANES), jnp.bfloat16),
            pltpu.VMEM(rl.shape, rl.dtype),
            pltpu.VMEM(rr.shape, rr.dtype),
            pltpu.VMEM((2, *weights.shape[1:]), weights.dtype),
            pltpu.VMEM((22, CH, LANES), jnp.float32),
            pltpu.VMEM((12, 4 * CH, LANES), jnp.bfloat16),
            *keep,
            pltpu.VMEM((8, LANES), jnp.float32),
            pltpu.SemaphoreType.DMA((12,)),
            pltpu.SemaphoreType.DMA((9,)),
        ],
        compiler_params=pltpu.CompilerParams(vmem_limit_bytes=62 << 20),
        cost_estimate=pl.CostEstimate(flops=8 << 30, bytes_accessed=8 << 20, transcendentals=0),
        name="first_convs",
    )(*pieces, rl, rr, weights)


def second_kernel_body(
    place, hid_in, hid_h_in, own_in, own_h_in, slope_in, slope_h_in, t_h_in, far_h_in,
    prev, following, a2, b2, w_in, after, out_ref,
    f_ref, w_ref, hid, hid_h, own_h, slope_ref, slope_h, t_h, far_h, img, img_h, pul, pul_h, sems,
):
    moves = [
        (w_in, w_ref),
        (t_h_in, t_h), (far_h_in, far_h),
        (prev, f_ref.at[0:7, 4:12]),
        (a2.at[0:7], f_ref.at[0:7, 0:4]),
        (b2.at[0:7], f_ref.at[0:7, 12:16]),
        (following, f_ref.at[7:14, 4:12]),
        (a2.at[7:14], f_ref.at[7:14, 0:4]),
        (b2.at[7:14], f_ref.at[7:14, 12:16]),
        (hid_in.at[2:8], hid.at[2:8]), (hid_h_in.at[2:8], hid_h.at[2:8]),
        (own_in, img.at[2:6, 2:10]), (own_h_in, own_h),
        (slope_in, slope_ref), (slope_h_in, slope_h),
    ]
    copies = [pltpu.make_async_copy(x, y, sems.at[i]) for i, (x, y) in enumerate(moves)]
    for copy in copies:
        copy.start()
    for copy in copies[:9]:
        copy.wait()

    def field_rows(t, r):
        return f_ref[t + 2, pl.ds(r, 4)].reshape(4 * CH, LANES)

    for i, m in enumerate(OUTER_LAYERS):

        def put(p, v):
            slope = f_ref[m, pl.ds(2 * p + 1, 2)].reshape(2 * CH, LANES)
            store(hid, m, p, slope.astype(jnp.float32) * v)

        def put_halo(v):
            store_halo(hid_h, m, far_h[i] * v)

        convolve_layer(w_ref[0], field_rows, lambda t: t_h[t], m, range(7), put, put_halo)

    for copy in copies[9:11]:
        copy.wait()
    wide = lax.broadcasted_iota(jnp.int32, (2 * CH, LANES), 1)
    wide8 = wide & 7
    gx, gy, gz = place[0], place[1], place[2]
    nx, ny, nz = place[3], place[4], place[5]
    top_in = jnp.where(gy > 0, 1.0, 0.0)
    low_in = jnp.where(gy < ny, 1.0, 0.0)
    halo_in = jnp.where(wide8 < 4, jnp.where(gz > 0, 1.0, 0.0), jnp.where(gz < nz, 1.0, 0.0))
    halo_in = jnp.where(wide < 8, halo_in * top_in, halo_in)
    halo_in = jnp.where(wide >= 40, halo_in * low_in, halo_in)

    def image_layer(m, x_in, pairs, merge):
        def put(p, v):
            keep = x_in * (top_in if p == 0 else low_in if p == 5 else 1.0)
            store(img, m, p, v * keep)

        def put_halo(v):
            store_halo(img_h, m, merge(v) * (halo_in * x_in))

        convolve_layer(w_ref[1], rows_of(hid), lambda t: hid_h[t], m, pairs, put, put_halo)

    def stage_ends(i, carry):
        m = jnp.where(i < 2, i, i + 4)
        x_in = jnp.where(((i >= 2) | (gx > 0)) & ((i < 2) | (gx < nx)), 1.0, 0.0)
        image_layer(m, x_in, range(6), lambda v: v)
        return carry

    lax.fori_loop(0, 4, stage_ends, 0, unroll=True)

    for copy in copies[11:]:
        copy.wait()

    def stage_rim(i, carry):
        m = i + 2
        outer = (wide < 8) | (wide >= 40)
        image_layer(m, 1.0, (0, 5), lambda v: jnp.where(outer, v, own_h[i]))
        return carry

    lax.fori_loop(0, 4, stage_rim, 0, unroll=True)

    def stage_pulled(m, carry):
        def put(p, v):
            slope = slope_ref[m, pl.ds(2 * p, 2)].reshape(2 * CH, LANES)
            store(pul, m, p, slope.astype(jnp.float32) * v)

        def put_halo(v):
            store_halo(pul_h, m, slope_h[m] * v)

        convolve_layer(w_ref[2], rows_of(img), lambda t: img_h[t], m, range(5), put, put_halo)
        return carry

    lax.fori_loop(0, 6, stage_pulled, 0, unroll=True)

    def stage_out(m, carry):
        def put(p, v):
            out_ref[m, pl.ds(2 * p, 2)] = v.reshape(2, CH, LANES)

        convolve_layer(w_ref[3], rows_of(pul), lambda t: pul_h[t], m, range(4), put, None)
        return carry

    lax.fori_loop(0, 4, stage_out, 0, unroll=True)


def second_convs(place, fields, outer, weights, after):
    return pl.pallas_call(
        second_kernel_body,
        out_shape=jax.ShapeDtypeStruct((4, 8, CH, LANES), jnp.float32),
        in_specs=[pl.BlockSpec(memory_space=pltpu.SMEM)]
        + [pl.BlockSpec(memory_space=pl.ANY)] * 14,
        scratch_shapes=[
            pltpu.VMEM((14, 16, CH, LANES), jnp.bfloat16),
            pltpu.VMEM(weights.shape, weights.dtype),
            *[pltpu.VMEM(f.shape, f.dtype) for i, f in enumerate(fields) if i != 2],
            pltpu.VMEM((8, 12, CH, LANES), jnp.bfloat16),
            pltpu.VMEM((8, 4 * CH, LANES), jnp.bfloat16),
            pltpu.VMEM((6, 10, CH, LANES), jnp.bfloat16),
            pltpu.VMEM((6, 4 * CH, LANES), jnp.bfloat16),
            pltpu.SemaphoreType.DMA((15,)),
        ],
        compiler_params=pltpu.CompilerParams(vmem_limit_bytes=62 << 20),
        cost_estimate=pl.CostEstimate(flops=8 << 30, bytes_accessed=4 << 20, transcendentals=0),
        name="second_convs",
    )(place, *fields, *outer, weights, after)


def weights_kernel(k1_ref, k2_ref, w_ref):
    w_ref[...] = jnp.zeros_like(w_ref)
    for which, (ref, adjoint) in enumerate(
        ((k1_ref, False), (k2_ref, False), (k2_ref, True), (k1_ref, True))
    ):
        for tap in range(27):
            a, b, c = tap // 9, tap // 3 % 3, tap % 3
            if adjoint:
                block = ref[26 - tap].astype(jnp.float32).T.astype(jnp.bfloat16)
            else:
                block = ref[tap]
            for row in range(2):
                top = (2 * c + row) * CH
                left = (4 * a + b + row) * CH
                w_ref[which, top : top + CH, left : left + CH] = block


def pair_matrices(first_kernel, second_kernel):
    return pl.pallas_call(
        weights_kernel,
        out_shape=jax.ShapeDtypeStruct((4, 6 * CH, 12 * CH), jnp.bfloat16),
        compiler_params=pltpu.CompilerParams(vmem_limit_bytes=8 << 20),
        cost_estimate=pl.CostEstimate(flops=0, bytes_accessed=4 << 20, transcendentals=0),
        name="pair_matrices",
    )(first_kernel, second_kernel)


def finish_kernel(result, parts, out_ref, norm_ref):
    total = jnp.sum(jnp.sum(parts[...], axis=0), axis=1, keepdims=True)
    norm = jnp.sqrt(total + 1e-06)
    norm_ref[0] = norm[0, 0]
    scale = jnp.broadcast_to(norm, (8, LANES))
    for x in range(result.shape[0]):
        out_ref[:, x] = result[x].transpose(1, 0, 2) / scale


def finish(result, parts):
    return pl.pallas_call(
        finish_kernel,
        out_shape=(
            jax.ShapeDtypeStruct((CH, 4, 8, LANES), jnp.float32),
            jax.ShapeDtypeStruct((1,), jnp.float32),
        ),
        out_specs=(
            pl.BlockSpec(memory_space=pltpu.VMEM),
            pl.BlockSpec(memory_space=pltpu.SMEM),
        ),
        compiler_params=pltpu.CompilerParams(vmem_limit_bytes=16 << 20),
        name="finish",
    )(result, parts)


def on_device(tangent, slopes, first_kernel, second_kernel):
    t = tangent.transpose(1, 2, 0, 3)
    s = slopes.transpose(1, 2, 0, 3)
    mine = jnp.concatenate([s[0:3], t, s[3:4]], axis=0)
    prev, following = shift_pair(mine[1:8], mine[0:7], "gx")
    a1, b1 = shift_pair(mine[:, 4:8], mine[:, 0:4], "gy")
    weights = pair_matrices(first_kernel, second_kernel)
    prev, following, a1, b1, weights = lax.optimization_barrier(
        (prev, following, a1, b1, weights)
    )
    low, top = edge_rows(prev, following)
    a2, b2 = shift_pair(low, top, "gy")
    left_edge, right_edge = pack_edges(a2, b2, pack_mid(prev, mine, following, a1, b1))
    rl, rr = shift_pair(right_edge, left_edge, "gz")
    plane = lax.axis_size(("gy", "gz"))
    pieces = (prev, mine, following, a1, b1, a2, b2)
    *fields, spread = first_convs(pieces, rl, rr, weights, plane)

    place = jnp.stack(
        [lax.axis_index(a) for a in ALL] + [jnp.int32(lax.axis_size(a) - 1) for a in ALL]
    ).astype(jnp.int32)
    parts = lax.all_to_all(spread, ("gy", "gz"), 0, 0, tiled=True)
    part = jnp.sum(parts, axis=0, keepdims=True)
    result = second_convs(place, fields, (prev, following, a2, b2), weights, part)
    count = lax.axis_size("gx")
    parts = lax.all_to_all(jnp.broadcast_to(part, (count, 1, LANES)), "gx", 0, 0, tiled=True)
    return finish(result, parts)


def solution(mesh):
    return jax.shard_map(
        on_device,
        mesh=mesh,
        in_specs=(P(None, "gx", "gy", "gz"), P(None, "gx", "gy", "gz"), P(), P()),
        out_specs=(P(None, "gx", "gy", "gz"), P()),
        check_vma=False,
    )
```

```python
import jax
import jax.numpy as jnp
from jax import lax
from jax.experimental import pallas as pl
from jax.experimental.pallas import tpu as pltpu
from jax.sharding import PartitionSpec as P

ALL = ("gx", "gy", "gz")
CH = 32
LANES = 128


def shift_pair(up, down, axis):
    ends = lax.axis_size(axis) - 1
    from_prev = lax.ppermute(up, axis, [(i, i + 1) for i in range(ends)])
    from_next = lax.ppermute(down, axis, [(i + 1, i) for i in range(ends)])
    return from_prev, from_next


def roll(v, shift):
    return pltpu.roll(v, shift % LANES, 1)


def slot_of(row):
    return 8 * (row % 2) + row // 2


def gather_edges(tile, rows, load, lane):
    for row in rows:
        slot = slot_of(row)
        rolled = roll(load(row).astype(jnp.float32), 8 * slot + 4)
        tile = jnp.where(lane // 8 == slot, rolled, tile)
    return tile


def rows_kernel(prev_ref, next_ref, low_ref, top_ref):
    low_ref[0:7] = prev_ref[:, 4:8]
    low_ref[7:14] = next_ref[:, 4:8]
    top_ref[0:7] = prev_ref[:, 0:4]
    top_ref[7:14] = next_ref[:, 0:4]


def edge_rows(prev, following):
    out = jax.ShapeDtypeStruct((14, 4, CH, LANES), jnp.bfloat16)
    return pl.pallas_call(
        rows_kernel,
        out_shape=(out, out),
        compiler_params=pltpu.CompilerParams(vmem_limit_bytes=16 << 20),
        cost_estimate=pl.CostEstimate(flops=0, bytes_accessed=1 << 21, transcendentals=0),
        name="edge_rows",
    )(prev, following)


OUTER = list(range(4)) + list(range(12, 16))


def pack_mid_kernel(prev_ref, mine_ref, next_ref, a1, b1, tile_ref):
    lane = lax.broadcasted_iota(jnp.int32, (CH, LANES), 1)
    none = jnp.zeros((CH, LANES), jnp.float32)

    def layers(ref, base):
        def body(i, carry):
            tile_ref[base + i] = gather_edges(none, range(4, 12), lambda r: ref[i, r - 4], lane)
            return carry

        lax.fori_loop(0, ref.shape[0], body, 0)

    def own(i, carry):
        def load(r):
            if 4 <= r < 12:
                return mine_ref[i, r - 4]
            return a1[i, r] if r < 4 else b1[i, r - 12]

        tile_ref[7 + i] = gather_edges(none, range(16), load, lane)
        return carry

    layers(prev_ref, 0)
    lax.fori_loop(0, 8, own, 0)
    layers(next_ref, 15)


def pack_mid(prev, mine, following, a1, b1):
    return pl.pallas_call(
        pack_mid_kernel,
        out_shape=jax.ShapeDtypeStruct((22, CH, LANES), jnp.float32),
        compiler_params=pltpu.CompilerParams(vmem_limit_bytes=16 << 20),
        cost_estimate=pl.CostEstimate(flops=0, bytes_accessed=1 << 21, transcendentals=0),
        name="pack_mid",
    )(prev, mine, following, a1, b1)


def pack_kernel(a2, b2, tile_ref, left_ref, right_ref, full):
    lane = lax.broadcasted_iota(jnp.int32, (CH, LANES), 1)
    low = (lane & 7) < 4
    full[7:15] = tile_ref[7:15]

    def received(i, carry):
        at = jnp.where(i < 7, i, i + 8)
        load = lambda r: a2[i, r] if r < 4 else b2[i, r - 12]
        full[at] = gather_edges(tile_ref[at], OUTER, load, lane)
        return carry

    lax.fori_loop(0, 14, received, 0, unroll=True)

    def group(g, carry):
        one, two = full[2 * g], full[2 * g + 1]
        right_ref[g] = jnp.where(low, one, roll(two, 4)).astype(jnp.bfloat16)
        left_ref[g] = jnp.where(low, roll(two, -4), one).astype(jnp.bfloat16)
        return carry

    lax.fori_loop(0, left_ref.shape[0], group, 0, unroll=True)


def pack_edges(a2, b2, tiles):
    out = jax.ShapeDtypeStruct((11, CH, LANES), jnp.bfloat16)
    return pl.pallas_call(
        pack_kernel,
        out_shape=(out, out),
        scratch_shapes=[pltpu.VMEM((22, CH, LANES), jnp.float32)],
        compiler_params=pltpu.CompilerParams(vmem_limit_bytes=16 << 20),
        cost_estimate=pl.CostEstimate(flops=0, bytes_accessed=1 << 21, transcendentals=0),
        name="pack_edges",
    )(a2, b2, tiles)


def convolve_layer(w, get, get_halo, m, pairs, put, put_halo):
    wide = lax.broadcasted_iota(jnp.int32, (2 * CH, LANES), 1)
    wide8 = wide & 7
    first = wide == 0
    n = 2 * CH

    def columns(p):
        if p < 0:
            return jnp.concatenate([get_halo(m + a) for a in range(3)], axis=0)
        return jnp.concatenate([get(m + a, 2 * p) for a in range(3)], axis=0)

    cross = None
    halo = None
    tiles = [-1] + list(pairs)
    for start in range(0, len(tiles), 2):
        here = tiles[start : start + 2]
        rhs = jnp.concatenate([columns(p) for p in here], axis=1)
        g = jnp.dot(w, rhs, preferred_element_type=jnp.float32)
        for k, p in enumerate(here):
            part = g[:, k * LANES : (k + 1) * LANES]
            before = roll(part[:n], 1)
            after = roll(part[2 * n :], -1)
            if p < 0:
                cross = jnp.where(wide8 == 4, before, after)
                halo = (
                    part[n : 2 * n]
                    + jnp.where(wide8 == 4, 0.0, before)
                    + jnp.where(wide8 == 3, 0.0, after)
                )
                continue
            mine = roll(cross, -(8 * p + 4))
            own = (
                part[n : 2 * n]
                + jnp.where(first, mine, before)
                + jnp.where(wide == LANES - 1, mine, after)
            )
            put(p, own)
            if put_halo is not None:
                give = roll(jnp.where(first, before, after), 8 * p + 4)
                halo = halo + jnp.where((wide == 8 * p + 3) | (wide == 8 * p + 4), give, 0.0)
    if put_halo is not None:
        put_halo(halo)


def store_halo(ref, m, v):
    for q, piece in enumerate((v[:CH], v[CH:], roll(v[:CH], -8), roll(v[CH:], -8))):
        ref[m, q * CH : (q + 1) * CH] = piece.astype(jnp.bfloat16)


def store(ref, m, p, v):
    ref[m, pl.ds(2 * p, 2)] = v.astype(jnp.bfloat16).reshape(2, CH, LANES)


def rows_of(ref):
    return lambda t, r: ref[t, pl.ds(r, 4)].reshape(4 * CH, LANES)


OUTER_LAYERS = (0, 1, 8, 9)


def first_kernel_body(
    prev, mine, following, a1, b1, a2, b2, rl_in, rr_in, w_in,
    hid_out, hid_h_out, own_out, own_h_out, slope_out, slope_h_out, t_h_out, far_h_out, sum_ref,
    f_ref, rl_ref, rr_ref, w_ref, edge, t_h, hid, hid_h, own_ref, own_h, slope_h, far_h, sum_acc, sems, out_sems,
):
    moves = [
        (rl_in, rl_ref),
        (rr_in, rr_ref),
        (w_in.at[0:2], w_ref),
        (prev, f_ref.at[0:7, 4:12]),
        (a2.at[0:7], f_ref.at[0:7, 0:4]),
        (b2.at[0:7], f_ref.at[0:7, 12:16]),
        (mine, f_ref.at[7:15, 4:12]),
        (a1, f_ref.at[7:15, 0:4]),
        (b1, f_ref.at[7:15, 12:16]),
        (following, f_ref.at[15:22, 4:12]),
        (a2.at[7:14], f_ref.at[15:22, 0:4]),
        (b2.at[7:14], f_ref.at[15:22, 12:16]),
    ]
    copies = [pltpu.make_async_copy(x, y, sems.at[i]) for i, (x, y) in enumerate(moves)]
    for copy in copies:
        copy.start()

    for copy in copies[:3]:
        copy.wait()
    lane = lax.broadcasted_iota(jnp.int32, (CH, LANES), 1)
    low = (lane & 7) < 4

    def unpack(g, carry):
        rl = rl_ref[g].astype(jnp.float32)
        rr = rr_ref[g].astype(jnp.float32)
        edge[2 * g] = jnp.where(low, rl, rr)
        edge[2 * g + 1] = jnp.where(low, roll(rl, -4), roll(rr, 4))
        return carry

    lax.fori_loop(0, rl_ref.shape[0], unpack, 0, unroll=True)

    def t_layer(t):
        return t + 2 + 4 * lax.shift_right_logical(t, 2)

    def s_layer(s):
        return s + 4 * lax.shift_right_logical(s + 2, 2)

    def t_halo(t, carry):
        tile = edge[t_layer(t)]
        for q, shift in enumerate((0, 64, -8, 56)):
            t_h[t, q * CH : (q + 1) * CH] = roll(tile, shift).astype(jnp.bfloat16)
        return carry

    lax.fori_loop(0, 12, t_halo, 0, unroll=True)

    def slope_halo(m, row):
        tile = edge[s_layer(m)]
        q = row // 2
        return jnp.concatenate([roll(tile, 64 - 8 * q), roll(tile, -8 * (q + 1))], axis=0)

    def keep_slopes(m, carry):
        slope_h[m] = slope_halo(m + 2, 3)
        return carry

    def field_rows(t, r):
        return f_ref[t_layer(t), pl.ds(r, 4)].reshape(4 * CH, LANES)

    lax.fori_loop(0, 6, keep_slopes, 0, unroll=True)
    for i, m in enumerate(OUTER_LAYERS):
        far_h[i] = slope_halo(m, 1)

    def stage_hidden(m, carry):
        def put(p, v):
            slope = f_ref[s_layer(m), pl.ds(2 * p + 1, 2)].reshape(2 * CH, LANES)
            store(hid, m, p, slope.astype(jnp.float32) * v)

        def put_halo(v):
            store_halo(hid_h, m, slope_halo(m, 1) * v)

        convolve_layer(w_ref[0], field_rows, lambda t: t_h[t], m, range(7), put, put_halo)
        return carry

    for start, end, first, last in ((2, 6, 3, 9), (6, 8, 9, 12)):
        for copy in copies[first:last]:
            copy.wait()
        lax.fori_loop(start, end, stage_hidden, 0, unroll=True)
    early = [
        (hid.at[2:8], hid_out.at[2:8]), (hid_h.at[2:8], hid_h_out.at[2:8]),
        (slope_h, slope_h_out), (t_h, t_h_out), (far_h, far_h_out),
        (f_ref.at[6:10, 3:13], slope_out.at[0:4]), (f_ref.at[14:16, 3:13], slope_out.at[4:6]),
    ]
    late = [(own_ref, own_out), (own_h, own_h_out)]
    writes = [pltpu.make_async_copy(x, y, out_sems.at[i]) for i, (x, y) in enumerate(early + late)]
    for copy in writes[:7]:
        copy.start()
    sum_acc[...] = jnp.zeros_like(sum_acc)

    def stage_own(m, carry):
        def put(p, v):
            own_ref[m, pl.ds(2 * p - 2, 2)] = v.astype(jnp.bfloat16).reshape(2, CH, LANES)
            square = v * v
            part = square[0:8]
            for q in range(1, 8):
                part = part + square[8 * q : 8 * q + 8]
            sum_acc[...] += part

        def put_halo(v):
            own_h[m] = v

        convolve_layer(
            w_ref[1], rows_of(hid), lambda t: hid_h[t], m + 2, range(1, 5), put, put_halo
        )
        return carry

    lax.fori_loop(0, 4, stage_own, 0, unroll=True)
    for copy in writes[7:]:
        copy.start()
    total = jnp.sum(sum_acc[...], axis=0, keepdims=True)
    for i in range(sum_ref.shape[0]):
        sum_ref[i] = total
    for copy in writes:
        copy.wait()


def first_convs(pieces, rl, rr, weights, spread):
    shape = jax.ShapeDtypeStruct
    anywhere = pl.BlockSpec(memory_space=pl.ANY)
    local = pl.BlockSpec(memory_space=pltpu.VMEM)
    fields = (
        shape((10, 14, CH, LANES), jnp.bfloat16),
        shape((10, 4 * CH, LANES), jnp.bfloat16),
        shape((4, 8, CH, LANES), jnp.bfloat16),
        shape((4, 2 * CH, LANES), jnp.float32),
        shape((6, 10, CH, LANES), jnp.bfloat16),
        shape((6, 2 * CH, LANES), jnp.float32),
        shape((12, 4 * CH, LANES), jnp.bfloat16),
        shape((4, 2 * CH, LANES), jnp.float32),
    )
    keep = [pltpu.VMEM(fields[i].shape, fields[i].dtype) for i in (0, 1, 2, 3, 5, 7)]
    return pl.pallas_call(
        first_kernel_body,
        out_shape=(*fields, shape((spread, 1, LANES), jnp.float32)),
        in_specs=[anywhere] * 10,
        out_specs=(*([anywhere] * 8), local),
        scratch_shapes=[
            pltpu.VMEM((22, 16, CH, LANES), jnp.bfloat16),
            pltpu.VMEM(rl.shape, rl.dtype),
            pltpu.VMEM(rr.shape, rr.dtype),
            pltpu.VMEM((2, *weights.shape[1:]), weights.dtype),
            pltpu.VMEM((22, CH, LANES), jnp.float32),
            pltpu.VMEM((12, 4 * CH, LANES), jnp.bfloat16),
            *keep,
            pltpu.VMEM((8, LANES), jnp.float32),
            pltpu.SemaphoreType.DMA((12,)),
            pltpu.SemaphoreType.DMA((9,)),
        ],
        compiler_params=pltpu.CompilerParams(vmem_limit_bytes=62 << 20),
        cost_estimate=pl.CostEstimate(flops=8 << 30, bytes_accessed=8 << 20, transcendentals=0),
        name="first_convs",
    )(*pieces, rl, rr, weights)


def second_kernel_body(
    place, hid_in, hid_h_in, own_in, own_h_in, slope_in, slope_h_in, t_h_in, far_h_in,
    prev, following, a2, b2, w_in, after, out_ref,
    f_ref, w_ref, hid, hid_h, own_h, slope_ref, slope_h, t_h, far_h, img, img_h, pul, pul_h, sems,
):
    moves = [
        (w_in, w_ref),
        (t_h_in, t_h), (far_h_in, far_h),
        (prev, f_ref.at[0:7, 4:12]),
        (a2.at[0:7], f_ref.at[0:7, 0:4]),
        (b2.at[0:7], f_ref.at[0:7, 12:16]),
        (following, f_ref.at[7:14, 4:12]),
        (a2.at[7:14], f_ref.at[7:14, 0:4]),
        (b2.at[7:14], f_ref.at[7:14, 12:16]),
        (hid_in.at[2:8], hid.at[2:8]), (hid_h_in.at[2:8], hid_h.at[2:8]),
        (own_in, img.at[2:6, 2:10]), (own_h_in, own_h),
        (slope_in, slope_ref), (slope_h_in, slope_h),
    ]
    copies = [pltpu.make_async_copy(x, y, sems.at[i]) for i, (x, y) in enumerate(moves)]
    for copy in copies:
        copy.start()
    for copy in copies[:9]:
        copy.wait()

    def field_rows(t, r):
        return f_ref[t + 2, pl.ds(r, 4)].reshape(4 * CH, LANES)

    for i, m in enumerate(OUTER_LAYERS):

        def put(p, v):
            slope = f_ref[m, pl.ds(2 * p + 1, 2)].reshape(2 * CH, LANES)
            store(hid, m, p, slope.astype(jnp.float32) * v)

        def put_halo(v):
            store_halo(hid_h, m, far_h[i] * v)

        convolve_layer(w_ref[0], field_rows, lambda t: t_h[t], m, range(7), put, put_halo)

    for copy in copies[9:11]:
        copy.wait()
    wide = lax.broadcasted_iota(jnp.int32, (2 * CH, LANES), 1)
    wide8 = wide & 7
    gx, gy, gz = place[0], place[1], place[2]
    nx, ny, nz = place[3], place[4], place[5]
    top_in = jnp.where(gy > 0, 1.0, 0.0)
    low_in = jnp.where(gy < ny, 1.0, 0.0)
    halo_in = jnp.where(wide8 < 4, jnp.where(gz > 0, 1.0, 0.0), jnp.where(gz < nz, 1.0, 0.0))
    halo_in = jnp.where(wide < 8, halo_in * top_in, halo_in)
    halo_in = jnp.where(wide >= 40, halo_in * low_in, halo_in)

    def image_layer(m, x_in, pairs, merge):
        def put(p, v):
            keep = x_in * (top_in if p == 0 else low_in if p == 5 else 1.0)
            store(img, m, p, v * keep)

        def put_halo(v):
            store_halo(img_h, m, merge(v) * (halo_in * x_in))

        convolve_layer(w_ref[1], rows_of(hid), lambda t: hid_h[t], m, pairs, put, put_halo)

    def stage_ends(i, carry):
        m = jnp.where(i < 2, i, i + 4)
        x_in = jnp.where(((i >= 2) | (gx > 0)) & ((i < 2) | (gx < nx)), 1.0, 0.0)
        image_layer(m, x_in, range(6), lambda v: v)
        return carry

    lax.fori_loop(0, 4, stage_ends, 0, unroll=True)

    for copy in copies[11:]:
        copy.wait()

    def stage_rim(i, carry):
        m = i + 2
        outer = (wide < 8) | (wide >= 40)
        image_layer(m, 1.0, (0, 5), lambda v: jnp.where(outer, v, own_h[i]))
        return carry

    lax.fori_loop(0, 4, stage_rim, 0, unroll=True)

    def stage_pulled(m, carry):
        def put(p, v):
            slope = slope_ref[m, pl.ds(2 * p, 2)].reshape(2 * CH, LANES)
            store(pul, m, p, slope.astype(jnp.float32) * v)

        def put_halo(v):
            store_halo(pul_h, m, slope_h[m] * v)

        convolve_layer(w_ref[2], rows_of(img), lambda t: img_h[t], m, range(5), put, put_halo)
        return carry

    lax.fori_loop(0, 6, stage_pulled, 0, unroll=True)

    def stage_out(m, carry):
        def put(p, v):
            out_ref[m, pl.ds(2 * p, 2)] = v.reshape(2, CH, LANES)

        convolve_layer(w_ref[3], rows_of(pul), lambda t: pul_h[t], m, range(4), put, None)
        return carry

    lax.fori_loop(0, 4, stage_out, 0, unroll=True)


def second_convs(place, fields, outer, weights, after):
    return pl.pallas_call(
        second_kernel_body,
        out_shape=jax.ShapeDtypeStruct((4, 8, CH, LANES), jnp.float32),
        in_specs=[pl.BlockSpec(memory_space=pltpu.SMEM)]
        + [pl.BlockSpec(memory_space=pl.ANY)] * 14,
        scratch_shapes=[
            pltpu.VMEM((14, 16, CH, LANES), jnp.bfloat16),
            pltpu.VMEM(weights.shape, weights.dtype),
            *[pltpu.VMEM(f.shape, f.dtype) for i, f in enumerate(fields) if i != 2],
            pltpu.VMEM((8, 12, CH, LANES), jnp.bfloat16),
            pltpu.VMEM((8, 4 * CH, LANES), jnp.bfloat16),
            pltpu.VMEM((6, 10, CH, LANES), jnp.bfloat16),
            pltpu.VMEM((6, 4 * CH, LANES), jnp.bfloat16),
            pltpu.SemaphoreType.DMA((15,)),
        ],
        compiler_params=pltpu.CompilerParams(vmem_limit_bytes=62 << 20),
        cost_estimate=pl.CostEstimate(flops=8 << 30, bytes_accessed=4 << 20, transcendentals=0),
        name="second_convs",
    )(place, *fields, *outer, weights, after)


def weights_kernel(k1_ref, k2_ref, w_ref):
    w_ref[...] = jnp.zeros_like(w_ref)
    for which, (ref, adjoint) in enumerate(
        ((k1_ref, False), (k2_ref, False), (k2_ref, True), (k1_ref, True))
    ):
        for tap in range(27):
            a, b, c = tap // 9, tap // 3 % 3, tap % 3
            if adjoint:
                block = ref[26 - tap].astype(jnp.float32).T.astype(jnp.bfloat16)
            else:
                block = ref[tap]
            for row in range(2):
                top = (2 * c + row) * CH
                left = (4 * a + b + row) * CH
                w_ref[which, top : top + CH, left : left + CH] = block


def pair_matrices(first_kernel, second_kernel):
    return pl.pallas_call(
        weights_kernel,
        out_shape=jax.ShapeDtypeStruct((4, 6 * CH, 12 * CH), jnp.bfloat16),
        compiler_params=pltpu.CompilerParams(vmem_limit_bytes=8 << 20),
        cost_estimate=pl.CostEstimate(flops=0, bytes_accessed=4 << 20, transcendentals=0),
        name="pair_matrices",
    )(first_kernel, second_kernel)


def turn_kernel(result, out_ref):
    for x in range(result.shape[0]):
        out_ref[:, x] = result[x].transpose(1, 0, 2)


def turn(result):
    return pl.pallas_call(
        turn_kernel,
        out_shape=jax.ShapeDtypeStruct((CH, 4, 8, LANES), jnp.float32),
        compiler_params=pltpu.CompilerParams(vmem_limit_bytes=16 << 20),
        cost_estimate=pl.CostEstimate(flops=0, bytes_accessed=4 << 20, transcendentals=0),
        name="turn",
    )(result)


def finish_kernel(block, parts, out_ref, norm_ref):
    total = jnp.sum(jnp.sum(parts[...], axis=0), axis=1, keepdims=True)
    norm = jnp.sqrt(total + 1e-06)
    norm_ref[0] = norm[0, 0]
    out_ref[...] = block[...] / jnp.broadcast_to(norm, (8, LANES))


def finish(block, parts):
    return pl.pallas_call(
        finish_kernel,
        out_shape=(
            jax.ShapeDtypeStruct(block.shape, jnp.float32),
            jax.ShapeDtypeStruct((1,), jnp.float32),
        ),
        out_specs=(
            pl.BlockSpec(memory_space=pltpu.VMEM),
            pl.BlockSpec(memory_space=pltpu.SMEM),
        ),
        compiler_params=pltpu.CompilerParams(vmem_limit_bytes=16 << 20),
        name="finish",
    )(block, parts)


def on_device(tangent, slopes, first_kernel, second_kernel):
    t = tangent.transpose(1, 2, 0, 3)
    s = slopes.transpose(1, 2, 0, 3)
    mine = jnp.concatenate([s[0:3], t, s[3:4]], axis=0)
    prev, following = shift_pair(mine[1:8], mine[0:7], "gx")
    a1, b1 = shift_pair(mine[:, 4:8], mine[:, 0:4], "gy")
    weights = pair_matrices(first_kernel, second_kernel)
    prev, following, a1, b1, weights = lax.optimization_barrier(
        (prev, following, a1, b1, weights)
    )
    low, top = edge_rows(prev, following)
    a2, b2 = shift_pair(low, top, "gy")
    left_edge, right_edge = pack_edges(a2, b2, pack_mid(prev, mine, following, a1, b1))
    rl, rr = shift_pair(right_edge, left_edge, "gz")
    plane = lax.axis_size(("gy", "gz"))
    pieces = (prev, mine, following, a1, b1, a2, b2)
    *fields, spread = first_convs(pieces, rl, rr, weights, plane)

    place = jnp.stack(
        [lax.axis_index(a) for a in ALL] + [jnp.int32(lax.axis_size(a) - 1) for a in ALL]
    ).astype(jnp.int32)
    parts = lax.all_to_all(spread, ("gy", "gz"), 0, 0, tiled=True)
    part = jnp.sum(parts, axis=0, keepdims=True)
    result = turn(second_convs(place, fields, (prev, following, a2, b2), weights, part))
    count = lax.axis_size("gx")
    parts = lax.all_to_all(jnp.broadcast_to(part, (count, 1, LANES)), "gx", 0, 0, tiled=True)
    return finish(result, parts)


def solution(mesh):
    return jax.shard_map(
        on_device,
        mesh=mesh,
        in_specs=(P(None, "gx", "gy", "gz"), P(None, "gx", "gy", "gz"), P(), P()),
        out_specs=(P(None, "gx", "gy", "gz"), P()),
        check_vma=False,
    )
```
